32 devices in a mesh: group: 2 (over y), context: 4 (over z), head: 4 (over x, core).
Axes of the slice: x: 2, y: 2, z: 4, core: 2. Of those that a mesh axis runs over, the one named last changes fastest.
Arguments:
- dn_query: bfloat16 [1024, 2048], P(('group', 'context'), 'head'), parts along dimension 0, may hold values from -6 to 6
- dn_key: bfloat16 [1024, 2048], P(('group', 'context'), 'head'), parts along dimension 0, may hold values from -6 to 6
- dn_value: bfloat16 [1024, 4096], P(('group', 'context'), 'head'), parts along dimension 0, may hold values from -6 to 6
- dn_gate: bfloat16 [1024, 4096], P(('group', 'context'), 'head'), parts along dimension 0, may hold values from -6 to 6
- dn_beta_logit: float32 [1024, 32], P(('group', 'context'), 'head'), parts along dimension 0, may hold values from -6 to 6
- dn_decay: float32 [1024, 32], P(('group', 'context'), 'head'), parts along dimension 0, may hold values from -1 to 0
- dn_norm_gain: float32 [128], replicated, may hold values from 0.1 to 1.9
- prefix_state: bfloat16 [4, 32, 128, 128], P('group', 'head', 'context'), parts along dimension 0, may hold values from -6 to 6
- at_query: bfloat16 [1024, 4096], P(('group', 'context'), 'head'), parts along dimension 0, may hold values from -6 to 6
- at_gate: bfloat16 [1024, 4096], P(('group', 'context'), 'head'), parts along dimension 0, may hold values from -6 to 6
- at_key: bfloat16 [1024, 512], P(('group', 'context')), parts along dimension 0, may hold values from -6 to 6
- at_value: bfloat16 [1024, 512], P(('group', 'context')), parts along dimension 0, may hold values from -6 to 6
- prefix_key: bfloat16 [16, 64, 512], P(('group', 'context')), parts along dimension 0, may hold values from -6 to 6
- prefix_value: bfloat16 [16, 64, 512], P(('group', 'context')), parts along dimension 0, may hold values from -6 to 6
- req_len: int32 [8], P('group'), parts along dimension 0, may hold values from 1 to 256, 512 in all
- req_prefix: int32 [8], P('group'), parts along dimension 0, may hold values from 0 to 1, as said below
- req_offset: int32 [8], P('group'), parts along dimension 0, may hold values from 64 to 256, as said below
- block_table: int32 [16], P('group'), parts along dimension 0, may hold values from 0 to 7, each once
Outputs:
- dn_out: bfloat16 [1024, 4096], P(('group', 'context'), 'head'), parts along dimension 0
- at_out: bfloat16 [1024, 4096], P(('group', 'context'), 'head'), parts along dimension 0
The draws below stay inside these ranges and needn't reach their ends.
There are 2 independent parts, one for each index of `group`. The reference program is written for one: setup_inputs(seed, part) draws one part's arguments, and reference() takes and returns one part's arrays. A program takes and returns all parts, laid end to end along the dimension named above; an argument that names none is the same for every part. Nothing has to cross between parts.
Inputs may be any that keep to these rules, and one draw needn't show every extreme that they name: `req_len`: requests lie one after another in row order; the longest has exactly 256 new tokens. `req_prefix`: every prefix is extended by one or more requests. `req_offset`: equal for the requests of one prefix: the number of its cached positions; one prefix holds 256, another from a quarter to a half of 256. `block_table`: entry p * 4 + j is the slot of block j of prefix p; every slot once.
All inputs are finite; a program needn't handle non-finite values.
Results may differ from the reference program's by a relative error of at most 0.011.
Values may be sent and summed in bfloat16 or wider, within the bound.
A program may use at most 128 MiB of HBM per device.

```python
import math
import jax
import jax.numpy as jnp
import numpy as np
from jax import lax

VH = 32
KH = 16
DK = 128
DV = 128
HQ = 16
KVH = 2
HD = 256
ROT = 64
TOK_DEV = 128
REQS = 4
PREF = 2
BLK = 64
NEW_ITEM_COUNT = 512
BLOCKS = 8
PBLK = 4
PLEN = 256
MOST = 256


def request_layout(key, part):
    base = jax.random.fold_in(key, 7101)
    order = jax.random.permutation(jax.random.fold_in(base, 1), REQS)
    spare = jax.random.randint(jax.random.fold_in(base, 2), (REQS,), 0, PREF)
    listed = jnp.where(jnp.arange(REQS) < PREF, jnp.arange(REQS) % PREF, spare)
    prefix = listed[order].astype(jnp.int32)
    sizes = jax.random.randint(jax.random.fold_in(base, 3), (PREF,), PLEN // 4, PLEN + 1)
    longest = prefix[0]
    shortest = (longest + 1 + jax.random.randint(jax.random.fold_in(base, 4), (), 0, PREF - 1)) % PREF
    half_span = max(PLEN // 4 // 2, 1)
    short_size = PLEN // 4 + 2 * jax.random.randint(jax.random.fold_in(base, 5), (), 0, half_span) + jnp.asarray(part, jnp.int32) % 2
    sizes = jnp.where(jnp.arange(PREF) == longest, PLEN, sizes)
    sizes = jnp.where(jnp.arange(PREF) == shortest, short_size, sizes)
    return (prefix, sizes[prefix].astype(jnp.int32))


def draw_req_prefix(key, part):
    return request_layout(key, part)[0]


def draw_req_offset(key, part):
    return request_layout(key, part)[1]


def draw_dn_decay(key, part):
    search_handles = jax.random.split(jax.random.fold_in(key, 3301), 7)
    fast_share = 0.5
    fast = jax.random.uniform(search_handles[0], (VH,)) < fast_share
    fast_rate = jnp.exp(jax.random.uniform(search_handles[1], (VH,), minval=math.log(1.0 / 50.0), maxval=math.log(1.0 / 30.0)))
    slow_rate = jnp.exp(jax.random.uniform(search_handles[2], (VH,), minval=math.log(0.1), maxval=0.0)) * math.log(10.0) / (4.0 * MOST)
    incoming_speed = jnp.where(fast, fast_rate, slow_rate)
    approximate_guess = jnp.exp(jax.random.uniform(search_handles[3], (NEW_ITEM_COUNT, VH), minval=math.log(0.7), maxval=math.log(1.4)))
    accelerator_scaling = jnp.exp(jax.random.uniform(search_handles[4], (NEW_ITEM_COUNT // TOK_DEV, 1, VH), minval=math.log(0.5), maxval=math.log(2.0)))
    accelerator_scaling = jnp.broadcast_to(accelerator_scaling, (NEW_ITEM_COUNT // TOK_DEV, TOK_DEV, VH)).reshape(NEW_ITEM_COUNT, VH)
    piece_waves = max(2, NEW_ITEM_COUNT // 1024)
    vacant_places = jax.random.randint(search_handles[5], (piece_waves,), 0, NEW_ITEM_COUNT)
    leading_absent = jnp.log(1.0 - jax.random.uniform(search_handles[6], (piece_waves,), minval=0.2, maxval=0.5))
    leading_found = (jnp.arange(NEW_ITEM_COUNT)[:, None] == vacant_places[None, :]).astype(jnp.float32)
    piece_wave = jnp.sum(leading_found * leading_absent[None, :], axis=1)
    return (-incoming_speed[None, :] * approximate_guess * accelerator_scaling + piece_wave[:, None]).astype(jnp.float32)


def drawn_values(key, heads):
    return jnp.clip(jax.random.normal(key, (NEW_ITEM_COUNT, heads, HD)), -6.0, 6.0)


def draw_at_query(key, part):
    drawn = drawn_values(jax.random.fold_in(key, 11), HQ)
    return drawn.reshape(NEW_ITEM_COUNT, HQ * HD).astype(jnp.bfloat16)


def draw_at_key(key, part):
    drawn = drawn_values(jax.random.fold_in(key, 12), KVH)
    return drawn.reshape(NEW_ITEM_COUNT, KVH * HD).astype(jnp.bfloat16)


def steps_of(own_key, dims, cuts, low, largest):
    def one(dim, blocks):
        draws = jax.random.uniform(jax.random.fold_in(jax.random.fold_in(own_key, 6), dim), (blocks,), jnp.float32, low / len(cuts), largest / len(cuts))
        return jnp.repeat(jnp.exp(draws), dims[dim] // blocks).reshape((-1,) + (1,) * (len(dims) - dim - 1))

    level = one(*cuts[0])
    for cut in cuts[1:]:
        level = level * one(*cut)
    return level


def split_up(amount, total, most, skew):
    loads = [(1 << 20) // math.isqrt(rank ** skew) + 1 for rank in range(2, amount + 1)]
    spare, given = total - most - (amount - 1), [1] * (amount - 1)
    while spare > 0:
        movable = [i for i in range(amount - 1) if given[i] < most]
        whole, remaining = sum([loads[i] for i in movable]), spare
        for i in movable:
            extra = min(most - given[i], max(1, remaining * loads[i] // whole), spare)
            given[i] = given[i] + extra
            spare = spare - extra
    return np.array([most] + given)


def ragged_sizes(rng, amount, total, most, slope):
    if amount == 2:
        one = jax.random.randint(rng, (), max(1, total - most), min(most, total - 1) + 1)
        return jnp.stack([one, total - one])
    tallies = jnp.asarray(split_up(amount, total, most, slope), jnp.int32)
    twos = (amount - 1) // 2
    source_of, receiver = tallies[1:1 + 2 * twos:2], tallies[2:2 + 2 * twos:2]
    slack = jnp.minimum(source_of - 1, most - receiver)
    moved = jax.random.randint(jax.random.fold_in(rng, 1), (twos,), 0, 1 << 20) % (slack + 1)
    tallies = tallies.at[1:1 + 2 * twos:2].set(source_of - moved).at[2:2 + 2 * twos:2].set(receiver + moved)
    return tallies[jax.random.permutation(jax.random.fold_in(rng, 2), amount)]


def gaussian(stream_key, dims, deviation, limit, pieces=(), held_as=jnp.bfloat16):
    factor_of = steps_of(stream_key, dims, pieces, -0.22, 0.18) if pieces else 1.0
    entries = jax.random.normal(stream_key, dims, jnp.float32) * deviation * factor_of
    return jnp.minimum(jnp.maximum(entries, -limit), limit).astype(held_as)


def setup_inputs(seed: int = 0, part: int = 0) -> dict:
    streams_of = jax.random.split(jax.random.key(seed), 19)
    own_keys = jax.random.split(jax.random.fold_in(streams_of[18], part), 19)
    dn_query = gaussian(own_keys[0], (NEW_ITEM_COUNT, KH * DK), 1.0, 6.0, ((0, 4), (1, 4)))
    dn_key = gaussian(own_keys[1], (NEW_ITEM_COUNT, KH * DK), 1.0, 6.0, ((0, 4), (1, 4)))
    dn_value = gaussian(own_keys[2], (NEW_ITEM_COUNT, VH * DV), 1.0, 6.0, ((0, 4), (1, 4)))
    dn_gate = gaussian(own_keys[3], (NEW_ITEM_COUNT, VH * DV), 1.0, 6.0, ((0, 4), (1, 4)))
    dn_beta_logit = gaussian(own_keys[4], (NEW_ITEM_COUNT, VH), 1.5, 6.0, ((0, 4), (1, 4)), jnp.float32)
    dn_decay = draw_dn_decay(jax.random.fold_in(jax.random.fold_in(streams_of[18], part), 71), part)
    dn_norm_gain = jnp.clip(1.0 + 0.18 * jax.random.normal(streams_of[6], (DV,), jnp.float32), 0.1, 1.9)
    prefix_state = gaussian(own_keys[7], (PREF, VH, DV, DK), 1.0, 6.0, ((1, 4), (2, 4)))
    at_query = draw_at_query(jax.random.fold_in(jax.random.fold_in(streams_of[18], part), 71), part)
    at_gate = gaussian(own_keys[9], (NEW_ITEM_COUNT, HQ * HD), 1.0, 6.0, ((0, 4), (1, 4)))
    at_key = draw_at_key(jax.random.fold_in(jax.random.fold_in(streams_of[18], part), 71), part)
    at_value = gaussian(own_keys[11], (NEW_ITEM_COUNT, KVH * HD), 1.0, 6.0, ((0, 4),))
    prefix_key = gaussian(own_keys[12], (BLOCKS, BLK, KVH * HD), 1.0, 6.0, ((0, 4),))
    prefix_value = gaussian(own_keys[13], (BLOCKS, BLK, KVH * HD), 1.0, 6.0, ((0, 4),))
    req_len = ragged_sizes(own_keys[14], REQS, NEW_ITEM_COUNT, MOST, 2).astype(jnp.int32)
    req_prefix = draw_req_prefix(jax.random.fold_in(jax.random.fold_in(streams_of[18], part), 71), part)
    req_offset = draw_req_offset(jax.random.fold_in(jax.random.fold_in(streams_of[18], part), 71), part)
    block_table = jax.random.permutation(own_keys[17], BLOCKS).astype(jnp.int32)
    return {"dn_query": dn_query, "dn_key": dn_key, "dn_value": dn_value, "dn_gate": dn_gate, "dn_beta_logit": dn_beta_logit, "dn_decay": dn_decay, "dn_norm_gain": dn_norm_gain, "prefix_state": prefix_state, "at_query": at_query, "at_gate": at_gate, "at_key": at_key, "at_value": at_value, "prefix_key": prefix_key, "prefix_value": prefix_value, "req_len": req_len, "req_prefix": req_prefix, "req_offset": req_offset, "block_table": block_table}


ROPE_THETA = 10000000.0
YARN_FACTOR = 4.0
YARN_ANCHOR = 262144.0
NEG_LARGE = -1e+30
HIGH = lax.Precision.HIGHEST

def yarn_tables(positions, rotary):
    half = rotary // 2
    log_theta = math.log(ROPE_THETA)
    lower = max(math.floor(rotary * math.log(YARN_ANCHOR / (64.0 * math.pi)) / (2.0 * log_theta)), 0)
    upper = min(math.ceil(rotary * math.log(YARN_ANCHOR / (2.0 * math.pi)) / (2.0 * log_theta)), rotary - 1)
    spread = float(upper - lower) if upper > lower else 0.001
    index = jnp.arange(half, dtype=jnp.float32)
    plain_frequency = jnp.exp(index * (-2.0 * log_theta / rotary))
    keep = 1.0 - jnp.clip((index - lower) / spread, 0.0, 1.0)
    frequency = plain_frequency * keep + plain_frequency / YARN_FACTOR * (1.0 - keep)
    angles = positions.astype(jnp.float32)[:, None] * frequency[None, :]
    attention_factor = 0.1 * math.log(YARN_FACTOR) + 1.0
    return (jnp.cos(angles) * attention_factor, jnp.sin(angles) * attention_factor)

def rotate(values, cosines, sines, rotary):
    half = rotary // 2
    first = values[..., :half]
    second = values[..., half:rotary]
    cosines = cosines[:, None, :]
    sines = sines[:, None, :]
    return jnp.concatenate([first * cosines - second * sines, second * cosines + first * sines, values[..., rotary:]], axis=-1)

def unit_rows(values):
    return values * lax.rsqrt(lax.optimization_barrier(jnp.sum(values * values, axis=-1, keepdims=True)) + 1e-06)

def row_layout(rows, req_len, req_prefix, req_offset):
    starts = (jnp.cumsum(req_len) - req_len).astype(jnp.int32)
    leading_found = (starts[None, :] <= rows[:, None]).astype(jnp.int32)
    segment = (lax.optimization_barrier(jnp.sum(leading_found, axis=1)) - 1).astype(jnp.int32)
    choose = (segment[:, None] == jnp.arange(req_len.shape[0], dtype=jnp.int32)[None, :]).astype(jnp.int32)
    first = lax.optimization_barrier(jnp.sum(choose * starts[None, :], axis=1)).astype(jnp.int32)
    prefix = lax.optimization_barrier(jnp.sum(choose * req_prefix[None, :], axis=1)).astype(jnp.int32)
    offset = lax.optimization_barrier(jnp.sum(choose * req_offset[None, :], axis=1)).astype(jnp.int32)
    return (segment, first, prefix, offset, (offset + rows - first).astype(jnp.int32))

def reference(dn_query, dn_key, dn_value, dn_gate, dn_beta_logit, dn_decay, dn_norm_gain, prefix_state, at_query, at_gate, at_key, at_value, prefix_key, prefix_value, req_len, req_prefix, req_offset, block_table):
    rows = jnp.arange(NEW_ITEM_COUNT, dtype=jnp.int32)
    segment, first, prefix, offset, position = row_layout(rows, req_len, req_prefix, req_offset)
    query = jnp.repeat(unit_rows(dn_query.reshape(NEW_ITEM_COUNT, KH, DK).astype(jnp.float32)) * DK ** (-0.5), VH // KH, axis=1)
    key = jnp.repeat(unit_rows(dn_key.reshape(NEW_ITEM_COUNT, KH, DK).astype(jnp.float32)), VH // KH, axis=1)
    value = dn_value.reshape(NEW_ITEM_COUNT, VH, DV).astype(jnp.float32)
    beta = jax.nn.sigmoid(dn_beta_logit)
    begins = rows == first
    identity = jnp.broadcast_to(jnp.eye(DK, dtype=jnp.float32), (VH, DK, DK))

    def advance(carry, inputs):
        state, transfer = carry
        query_row, key_row, value_row, beta_row, decay_row, begin_row = inputs
        state = jnp.where(begin_row, jnp.zeros_like(state), state)
        transfer = jnp.where(begin_row, identity, transfer)
        factor = jnp.exp(decay_row)[:, None, None]
        strength = beta_row[:, None, None]
        state_key = jnp.einsum('hvk,hk->hv', state, key_row, precision=HIGH)
        state = factor * (state - strength * state_key[:, :, None] * key_row[:, None, :]) + strength * value_row[:, :, None] * key_row[:, None, :]
        transfer_key = jnp.einsum('hjk,hk->hj', transfer, key_row, precision=HIGH)
        transfer = factor * (transfer - strength * transfer_key[:, :, None] * key_row[:, None, :])
        local_row = jnp.einsum('hvk,hk->hv', state, query_row, precision=HIGH)
        reach_row = jnp.einsum('hjk,hk->hj', transfer, query_row, precision=HIGH)
        return ((state, transfer), (local_row, reach_row))
    initial = (jnp.zeros((VH, DV, DK), jnp.float32), identity)
    unused, (local_out, reach) = lax.scan(advance, initial, (query, key, value, beta, dn_decay, begins))
    weights = reach.astype(jnp.bfloat16)

    def state_term(block):
        owners = lax.dynamic_slice_in_dim(prefix, block * 8, 8)
        vectors = lax.dynamic_slice_in_dim(weights, block * 8, 8, 0)
        states = jnp.take(prefix_state, owners, axis=0).astype(jnp.float32)
        return jnp.einsum('thvk,thk->thv', states, vectors.astype(jnp.float32), precision=HIGH)
    carried = lax.map(state_term, jnp.arange(NEW_ITEM_COUNT // 8, dtype=jnp.int32)).reshape(NEW_ITEM_COUNT, VH, DV)
    core = local_out + carried
    normed = core * lax.rsqrt(lax.optimization_barrier(jnp.mean(core * core, axis=-1, keepdims=True)) + 1e-06)
    gate = dn_gate.reshape(NEW_ITEM_COUNT, VH, DV).astype(jnp.float32)
    dn_out = (normed * dn_norm_gain * jax.nn.silu(gate)).reshape(NEW_ITEM_COUNT, VH * DV).astype(jnp.bfloat16)
    cosines, sines = yarn_tables(position, ROT)
    group = HQ // KVH
    query_rot = rotate(at_query.reshape(NEW_ITEM_COUNT, HQ, HD).astype(jnp.float32), cosines, sines, ROT).astype(jnp.bfloat16)
    query_rot = query_rot.reshape(NEW_ITEM_COUNT, KVH, group, HD)
    key_rot = rotate(at_key.reshape(NEW_ITEM_COUNT, KVH, HD).astype(jnp.float32), cosines, sines, ROT).astype(jnp.bfloat16)
    value_new = at_value.reshape(NEW_ITEM_COUNT, KVH, HD)
    order = block_table.reshape(PREF * PBLK)
    cached_keys = jnp.take(prefix_key, order, axis=0).reshape(PREF * PLEN, KVH, HD).astype(jnp.float32)
    cached_values = jnp.take(prefix_value, order, axis=0).reshape(PREF * PLEN, KVH, HD).astype(jnp.float32)
    flat_index = jnp.arange(PREF * PLEN, dtype=jnp.int32)
    flat_owner = flat_index // PLEN
    flat_place = flat_index % PLEN
    padded_keys = jnp.concatenate([jnp.zeros((MOST, KVH, HD), jnp.bfloat16), key_rot], axis=0)
    padded_values = jnp.concatenate([jnp.zeros((MOST, KVH, HD), jnp.bfloat16), value_new], axis=0)
    padded_segment = jnp.concatenate([jnp.full((MOST,), -1, jnp.int32), segment])
    window = MOST + TOK_DEV - 1
    scale = HD ** (-0.5)

    def attend(block):
        begin = block * TOK_DEV
        queries = lax.dynamic_slice_in_dim(query_rot, begin, TOK_DEV, 0).astype(jnp.float32)
        owners = lax.dynamic_slice_in_dim(prefix, begin, TOK_DEV)
        limits = lax.dynamic_slice_in_dim(offset, begin, TOK_DEV)
        own_segment = lax.dynamic_slice_in_dim(segment, begin, TOK_DEV)
        own_rows = begin + jnp.arange(TOK_DEV, dtype=jnp.int32)
        near_keys = lax.dynamic_slice_in_dim(padded_keys, begin + 1, window, 0).astype(jnp.float32)
        near_values = lax.dynamic_slice_in_dim(padded_values, begin + 1, window, 0).astype(jnp.float32)
        near_segment = lax.dynamic_slice_in_dim(padded_segment, begin + 1, window)
        near_rows = begin + 1 - MOST + jnp.arange(window, dtype=jnp.int32)
        old_scores = jnp.einsum('tkgd,nkd->tkgn', queries, cached_keys, precision=HIGH) * scale
        new_scores = jnp.einsum('tkgd,nkd->tkgn', queries, near_keys, precision=HIGH) * scale
        old_mask = (flat_owner[None, :] == owners[:, None]) & (flat_place[None, :] < limits[:, None])
        old_seen = jnp.broadcast_to(old_mask[:, None, None, :], old_scores.shape)
        new_mask = (near_segment[None, :] == own_segment[:, None]) & (near_rows[None, :] <= own_rows[:, None])
        new_seen = jnp.broadcast_to(new_mask[:, None, None, :], new_scores.shape)
        peak = jnp.maximum(lax.optimization_barrier(jnp.max(jnp.where(old_seen, old_scores, NEG_LARGE), axis=-1)), lax.optimization_barrier(jnp.max(jnp.where(new_seen, new_scores, NEG_LARGE), axis=-1)))[..., None]
        old_numer = jnp.where(old_seen, jnp.exp(old_scores - peak), 0.0)
        new_numer = jnp.where(new_seen, jnp.exp(new_scores - peak), 0.0)
        total = lax.optimization_barrier(jnp.sum(old_numer, axis=-1)) + lax.optimization_barrier(jnp.sum(new_numer, axis=-1))
        old_round = lax.optimization_barrier(old_numer.astype(jnp.bfloat16)).astype(jnp.float32)
        new_round = lax.optimization_barrier(new_numer.astype(jnp.bfloat16)).astype(jnp.float32)
        summed = jnp.einsum('tkgn,nkd->tkgd', old_round, cached_values, precision=HIGH)
        summed = summed + jnp.einsum('tkgn,nkd->tkgd', new_round, near_values, precision=HIGH)
        return summed / total[..., None]
    attention = lax.map(attend, jnp.arange(NEW_ITEM_COUNT // TOK_DEV, dtype=jnp.int32)).reshape(NEW_ITEM_COUNT, HQ, HD)
    gate_att = at_gate.reshape(NEW_ITEM_COUNT, HQ, HD).astype(jnp.float32)
    at_out = (attention * jax.nn.sigmoid(gate_att)).reshape(NEW_ITEM_COUNT, HQ * HD).astype(jnp.bfloat16)
    return (dn_out, at_out)
```

```python
import math

import jax
import jax.numpy as jnp
from jax import lax
from jax.experimental import pallas as pl
from jax.experimental.pallas import tpu as pltpu
from jax.sharding import PartitionSpec as P

VH = 32
KH = 16
DK = 128
DV = 128
HQ = 16
KVH = 2
HD = 256
ROT = 64


ROPE_THETA = 10000000.0
YARN_FACTOR = 4.0
YARN_ANCHOR = 262144.0
NEG_LARGE = -1e30
HIGH = lax.Precision.HIGHEST


def exchange_kernel(count, size, later_only, *refs):
    sources, targets = refs[:count], refs[count : 2 * count]
    send_sem, recv_sem, own_sem = refs[2 * count :]
    me = lax.axis_index("context")
    barrier = pltpu.get_barrier_semaphore()
    for step in range(1, size):
        pl.semaphore_signal(barrier, inc=1, device_id={"context": lax.rem(me + step, size)})
    pl.semaphore_wait(barrier, size - 1)

    def sent(step, which):
        return pltpu.make_async_remote_copy(
            src_ref=sources[which],
            dst_ref=targets[which].at[me],
            send_sem=send_sem.at[which, step - 1],
            recv_sem=recv_sem.at[which, step - 1],
            device_id={"context": lax.rem(me + step, size)},
        )

    own = [
        pltpu.make_async_copy(sources[which], targets[which].at[me], own_sem.at[which])
        for which in range(count)
    ]
    for step in range(1, size):

        def begin(step=step):
            for which in range(count):
                sent(step, which).start()

        if later_only:
            pl.when(me + step < size)(begin)
        else:
            begin()
    for copy in own:
        copy.start()
    for step in range(1, size):

        def end_send(step=step):
            for which in range(count):
                sent(step, which).wait_send()

        def end_recv(step=step):
            for which in range(count):
                sent(step, which).wait_recv()

        if later_only:
            pl.when(me + step < size)(end_send)
            pl.when(me >= step)(end_recv)
        else:
            end_send()
            end_recv()
    for copy in own:
        copy.wait()


def exchange(arrays, size, number, later_only=False):
    count = len(arrays)
    return pl.pallas_call(
        lambda *refs: exchange_kernel(count, size, later_only, *refs),
        out_shape=[jax.ShapeDtypeStruct((size,) + a.shape, a.dtype) for a in arrays],
        in_specs=[pl.BlockSpec(memory_space=pl.ANY)] * count,
        out_specs=[pl.BlockSpec(memory_space=pl.ANY)] * count,
        scratch_shapes=[
            pltpu.SemaphoreType.DMA((count, size - 1)),
            pltpu.SemaphoreType.DMA((count, size - 1)),
            pltpu.SemaphoreType.DMA((count,)),
        ],
        compiler_params=pltpu.CompilerParams(collective_id=number, has_side_effects=True),
    )(*arrays)


def unit_lower_inverse(lower):
    size = lower.shape[-1]
    index = jnp.arange(size)
    inverse = jnp.eye(size, dtype=jnp.float32)[None] - jnp.where(
        (index[:, None] // 2 == index[None, :] // 2)[None], lower, 0.0
    )
    width = 2
    while width < size:
        block = index // width
        pair = (block[:, None] // 2 == block[None, :] // 2) & (block[:, None] > block[None, :])
        cross = jnp.where(pair[None], lower, 0.0)
        half = jnp.einsum("hij,hjk->hik", cross, inverse, precision=HIGH)
        inverse = inverse - jnp.einsum("hij,hjk->hik", inverse, half, precision=HIGH)
        width *= 2
    return inverse


def yarn_tables(positions, rotary):
    half = rotary // 2
    log_theta = math.log(ROPE_THETA)
    lower = max(
        math.floor(rotary * math.log(YARN_ANCHOR / (64.0 * math.pi)) / (2.0 * log_theta)), 0
    )
    upper = min(
        math.ceil(rotary * math.log(YARN_ANCHOR / (2.0 * math.pi)) / (2.0 * log_theta)), rotary - 1
    )
    spread = float(upper - lower)
    index = jnp.arange(half, dtype=jnp.float32)
    plain_frequency = jnp.exp(index * (-2.0 * log_theta / rotary))
    keep = 1.0 - jnp.clip((index - lower) / spread, 0.0, 1.0)
    frequency = plain_frequency * keep + plain_frequency / YARN_FACTOR * (1.0 - keep)
    angles = positions.astype(jnp.float32)[:, None] * frequency[None, :]
    attention_factor = 0.1 * math.log(YARN_FACTOR) + 1.0
    return (jnp.cos(angles) * attention_factor, jnp.sin(angles) * attention_factor)


def rotate(values, cosines, sines, rotary):
    half = rotary // 2
    first = values[..., :half]
    second = values[..., half:rotary]
    cosines = cosines[:, None, :]
    sines = sines[:, None, :]
    return jnp.concatenate(
        [first * cosines - second * sines, second * cosines + first * sines, values[..., rotary:]],
        axis=-1,
    )


def unit_rows(values):
    return values * lax.rsqrt(jnp.sum(values * values, axis=-1, keepdims=True) + 1e-06)


def row_layout(rows, req_len, req_prefix, req_offset):
    starts = jnp.cumsum(req_len) - req_len
    leading_found = (starts[None, :] <= rows[:, None]).astype(jnp.int32)
    segment = jnp.sum(leading_found, axis=1) - 1
    choose = (segment[:, None] == jnp.arange(req_len.shape[0], dtype=jnp.int32)[None, :]).astype(
        jnp.int32
    )
    first = jnp.sum(choose * starts[None, :], axis=1)
    prefix = jnp.sum(choose * req_prefix[None, :], axis=1)
    offset = jnp.sum(choose * req_offset[None, :], axis=1)
    return (segment, first, prefix, offset, offset + rows - first)


def absorb(state, queries, search_handles, values, visible):
    peak, total, summed = state
    scores = jnp.einsum(
        "thd,nd->thn", queries, search_handles, preferred_element_type=jnp.float32
    ) * search_handles.shape[-1] ** (-0.5)
    seen = visible[:, None, :]
    scores = jnp.where(seen, scores, NEG_LARGE)
    new_peak = jnp.maximum(peak, jnp.max(scores, axis=-1))
    weights = jnp.where(seen, jnp.exp(scores - new_peak[..., None]), 0.0)
    shrink = jnp.exp(peak - new_peak)
    total = total * shrink + jnp.sum(weights, axis=-1)
    summed = summed * shrink[..., None] + jnp.einsum(
        "thn,nd->thd", weights.astype(jnp.bfloat16), values, preferred_element_type=jnp.float32
    )
    return (new_peak, total, summed)


def shards(
    dn_query,
    dn_key,
    dn_value,
    dn_gate,
    dn_beta_logit,
    dn_decay,
    dn_norm_gain,
    prefix_state,
    at_query,
    at_gate,
    at_key,
    at_value,
    prefix_key,
    prefix_value,
    req_len,
    req_prefix,
    req_offset,
    block_table,
):
    tokens_here = dn_query.shape[0]
    key_heads = dn_query.shape[1] // DK
    value_heads = dn_value.shape[1] // DV
    query_heads = at_query.shape[1] // HD
    device = lax.axis_index("context")
    row_start = device * tokens_here
    rows = row_start + jnp.arange(tokens_here, dtype=jnp.int32)
    segment, first, prefix, offset, position = row_layout(rows, req_len, req_prefix, req_offset)
    size = lax.axis_size("context")
    query_heads_here = query_heads
    kv_head = lax.axis_index("head") * query_heads_here // (HQ // KVH)
    cosines, sines = yarn_tables(position, ROT)
    new_key = lax.dynamic_slice_in_dim(at_key, kv_head * HD, HD, 1).reshape(tokens_here, 1, HD)
    new_key = (
        rotate(new_key.astype(jnp.float32), cosines, sines, ROT)
        .reshape(tokens_here, HD)
        .astype(jnp.bfloat16)
    )
    new_value = lax.dynamic_slice_in_dim(at_value, kv_head * HD, HD, 1)
    cached_key = lax.dynamic_slice_in_dim(prefix_key, kv_head * HD, HD, 2)
    cached_value = lax.dynamic_slice_in_dim(prefix_value, kv_head * HD, HD, 2)
    states, old_keys, old_values, new_keys, new_values = exchange(
        [prefix_state, cached_key, cached_value, new_key, new_value], size, 0
    )
    states = jnp.moveaxis(states, 0, 2)
    states = states.reshape(states.shape[:2] + (-1, DK))
    old_keys = old_keys.reshape((-1,) + old_keys.shape[2:])
    old_values = old_values.reshape((-1,) + old_values.shape[2:])
    new_keys = new_keys.reshape(-1, HD)
    new_values = new_values.reshape(-1, HD)
    query = jnp.repeat(
        unit_rows(dn_query.reshape(tokens_here, key_heads, DK).astype(jnp.float32)) * DK ** (-0.5),
        VH // KH,
        axis=1,
    )
    key = jnp.repeat(
        unit_rows(dn_key.reshape(tokens_here, key_heads, DK).astype(jnp.float32)), VH // KH, axis=1
    )
    query_heads_first = jnp.transpose(query, (1, 0, 2))
    key_heads_first = jnp.transpose(key, (1, 0, 2))
    value_heads_first = jnp.transpose(
        dn_value.reshape(tokens_here, value_heads, DV).astype(jnp.float32), (1, 0, 2)
    )
    beta = jax.nn.sigmoid(dn_beta_logit).T
    same = segment[:, None] == segment[None, :]
    causal = same & (rows[:, None] >= rows[None, :])
    strict = same & (rows[:, None] > rows[None, :])
    running = jnp.dot(causal.astype(jnp.float32), dn_decay, precision=HIGH).T
    gaps = running[:, :, None] - running[:, None, :]
    decay_mat = jnp.where(causal[None], jnp.exp(jnp.where(causal[None], gaps, 0.0)), 0.0)
    key_gram = jnp.einsum("hid,hjd->hij", key_heads_first, key_heads_first, precision=HIGH)
    query_key = jnp.einsum("hid,hjd->hij", query_heads_first, key_heads_first, precision=HIGH)
    lower_mat = jnp.where(strict[None], beta[:, :, None] * key_gram * decay_mat, 0.0)
    start_decay = jnp.exp(running)
    solve_values = beta[:, :, None] * value_heads_first
    solve_keys = (beta * start_decay)[:, :, None] * key_heads_first
    solved = jnp.einsum(
        "hij,hjk->hik",
        unit_lower_inverse(lower_mat),
        jnp.concatenate([solve_values, solve_keys], axis=2),
        precision=HIGH,
    )
    update = solved[:, :, :DV]
    wy_keys = solved[:, :, DV:]
    mixing = decay_mat * query_key
    local_out = jnp.einsum("hij,hjv->hiv", mixing, update, precision=HIGH)
    reach = start_decay[:, :, None] * query_heads_first - jnp.einsum(
        "hij,hjk->hik", mixing, wy_keys, precision=HIGH
    )
    tail = segment == segment[tokens_here - 1]
    end_gaps = running[:, tokens_here - 1 : tokens_here] - running
    end_weight = jnp.where(tail[None, :], jnp.exp(jnp.where(tail[None, :], end_gaps, 0.0)), 0.0)
    end_decay = start_decay[:, tokens_here - 1]
    identity_mat = jnp.eye(DK, dtype=jnp.float32)
    carry_map = end_decay[:, None, None] * identity_mat[None] - jnp.einsum(
        "hjk,hj,hjl->hkl", wy_keys, end_weight, key_heads_first, precision=HIGH
    )
    carry_add = jnp.einsum("hjv,hj,hjl->hvl", update, end_weight, key_heads_first, precision=HIGH)
    map_all, add_all = exchange(
        [carry_map.astype(jnp.bfloat16), carry_add.astype(jnp.bfloat16)], size, 1, True
    )
    starts = jnp.cumsum(req_len) - req_len
    into_map = jnp.broadcast_to(identity_mat, (value_heads, DK, DK))
    into_add = jnp.zeros((value_heads, DV, DK), jnp.float32)
    for turn in range(size - 1):
        low, high = turn * tokens_here, (turn + 1) * tokens_here
        fresh = jnp.any((starts >= low) & (starts < high))
        used = turn < device
        map_one = jnp.where(used, map_all[turn], 0).astype(jnp.float32)
        add_one = jnp.where(used, add_all[turn], 0).astype(jnp.float32)
        if turn == 0:
            next_map, next_add = map_one, add_one
        else:
            both = jnp.einsum(
                "hij,hjk->hik",
                jnp.concatenate([into_map, into_add], axis=1),
                map_one,
                precision=HIGH,
            )
            next_map = jnp.where(fresh, map_one, both[:, :DK])
            next_add = jnp.where(fresh, 0.0, both[:, DK:]) + add_one
        into_map = jnp.where(used, next_map, into_map)
        into_add = jnp.where(used, next_add, into_add)
    carried = ((segment == segment[0]) & (first[0] < row_start))[None, :, None]
    through = jnp.einsum("hkl,hil->hik", into_map, reach, precision=HIGH)
    extra = jnp.einsum("hvk,hik->hiv", into_add, reach, precision=HIGH)
    weight_vec = jnp.where(carried, through, reach).astype(jnp.bfloat16)
    core = local_out + jnp.where(carried, extra, 0.0)
    owner_ids = jnp.arange(prefix_state.shape[0], dtype=jnp.int32)
    select = (prefix[None, :] == owner_ids[:, None]).astype(jnp.bfloat16)
    masked = select[:, None, :, None] * weight_vec[None]
    state_part = jnp.einsum(
        "phik,phvk->hiv",
        masked,
        states,
        preferred_element_type=jnp.float32,
    )
    core = core + state_part
    core_rows = jnp.transpose(core, (1, 0, 2))
    normed = core_rows * lax.rsqrt(jnp.mean(core_rows * core_rows, axis=-1, keepdims=True) + 1e-06)
    gate_rows = dn_gate.reshape(tokens_here, value_heads, DV).astype(jnp.float32)
    dn_out = (
        (normed * dn_norm_gain * jax.nn.silu(gate_rows))
        .reshape(tokens_here, value_heads * DV)
        .astype(jnp.bfloat16)
    )
    query_rot = rotate(
        at_query.reshape(tokens_here, query_heads, HD).astype(jnp.float32), cosines, sines, ROT
    ).astype(jnp.bfloat16)
    table_index = jnp.arange(block_table.shape[0], dtype=jnp.int32)
    blocks_per_prefix = block_table.shape[0] // prefix_state.shape[0]
    state = (
        jnp.full((tokens_here, query_heads), NEG_LARGE, jnp.float32),
        jnp.zeros((tokens_here, query_heads), jnp.float32),
        jnp.zeros((tokens_here, query_heads, HD), jnp.float32),
    )
    search_handles = old_keys
    values = old_values
    count = search_handles.shape[0]
    width = search_handles.shape[1]
    slots = jnp.arange(count, dtype=jnp.int32)
    entry = jnp.sum(
        jnp.where(block_table[None, :] == slots[:, None], table_index[None, :], 0), axis=1
    )
    owner = jnp.repeat(entry // blocks_per_prefix, width)
    where_in = (
        (entry % blocks_per_prefix)[:, None] * width + jnp.arange(width, dtype=jnp.int32)[None, :]
    ).reshape(count * width)
    visible = (owner[None, :] == prefix[:, None]) & (where_in[None, :] < offset[:, None])
    flat_keys = search_handles.reshape(count * width, search_handles.shape[2])
    flat_values = values.reshape(count * width, values.shape[2])
    state = absorb(state, query_rot, flat_keys, flat_values, visible)
    search_handles = new_keys
    values = new_values
    key_rows = jnp.arange(search_handles.shape[0], dtype=jnp.int32)
    key_segment = row_layout(key_rows, req_len, req_prefix, req_offset)[0]
    visible = (key_segment[None, :] == segment[:, None]) & (key_rows[None, :] <= rows[:, None])
    state = absorb(state, query_rot, search_handles, values, visible)
    peak, total, summed = state
    attention = summed / total[..., None]
    gate_att = at_gate.reshape(tokens_here, query_heads, HD).astype(jnp.float32)
    at_out = (
        (attention * jax.nn.sigmoid(gate_att))
        .reshape(tokens_here, query_heads * HD)
        .astype(jnp.bfloat16)
    )
    return (dn_out, at_out)


def solution(mesh):
    placed = (
        P(("group", "context"), "head"),
        P(("group", "context"), "head"),
        P(("group", "context"), "head"),
        P(("group", "context"), "head"),
        P(("group", "context"), "head"),
        P(("group", "context"), "head"),
        P(),
        P("group", "head", "context", None),
        P(("group", "context"), "head"),
        P(("group", "context"), "head"),
        P(("group", "context"), None),
        P(("group", "context"), None),
        P(("group", "context"), None, None),
        P(("group", "context"), None, None),
        P("group"),
        P("group"),
        P("group"),
        P("group"),
    )
    return jax.shard_map(
        shards,
        mesh=mesh,
        in_specs=placed,
        out_specs=(P(("group", "context"), "head"), P(("group", "context"), "head")),
        check_vma=False,
    )
```

```python
import math

import jax
import jax.numpy as jnp
from jax import lax
from jax.experimental import pallas as pl
from jax.experimental.pallas import tpu as pltpu
from jax.sharding import PartitionSpec as P

VH = 32
KH = 16
DK = 128
DV = 128
HQ = 16
KVH = 2
HD = 256
ROT = 64


ROPE_THETA = 10000000.0
YARN_FACTOR = 4.0
YARN_ANCHOR = 262144.0
NEG_LARGE = -1e30
HIGH = lax.Precision.HIGHEST


def chain_kernel(size, map_ref, add_ref, into_ref, held, leaving, send_sem, recv_sem):
    me = lax.axis_index("context")
    heads = map_ref.shape[0]
    barrier = pltpu.get_barrier_semaphore()
    after, before = lax.rem(me + 1, size), lax.rem(me + size - 1, size)
    for neighbour in (before, after):
        pl.semaphore_signal(barrier, inc=1, device_id={"context": neighbour})
    pl.semaphore_wait(barrier, 2)

    def sent(h):
        return pltpu.make_async_remote_copy(
            src_ref=leaving.at[h],
            dst_ref=held.at[h],
            send_sem=send_sem.at[h],
            recv_sem=recv_sem.at[h],
            device_id={"context": after},
        )

    @pl.when(me == 0)
    def _():
        held[...] = jnp.zeros_like(held)

    for h in range(heads):

        @pl.when(me > 0)
        def _(h=h):
            sent(h).wait_recv()

        leaving[h] = (
            jnp.dot(held[h], map_ref[h], preferred_element_type=jnp.float32) + add_ref[h]
        ).astype(jnp.bfloat16)

        @pl.when(me < size - 1)
        def _(h=h):
            sent(h).start()

    into_ref[...] = held[...]

    @pl.when(me < size - 1)
    def _():
        for h in range(heads):
            sent(h).wait_send()


def chain(carry_map, carry_add, size):
    heads = carry_map.shape[0]
    return pl.pallas_call(
        lambda *refs: chain_kernel(size, *refs),
        out_shape=jax.ShapeDtypeStruct(carry_add.shape, jnp.bfloat16),
        in_specs=[pl.BlockSpec(memory_space=pltpu.VMEM)] * 2,
        out_specs=pl.BlockSpec(memory_space=pltpu.VMEM),
        scratch_shapes=[
            pltpu.VMEM(carry_add.shape, jnp.bfloat16),
            pltpu.VMEM(carry_add.shape, jnp.bfloat16),
            pltpu.SemaphoreType.DMA((heads,)),
            pltpu.SemaphoreType.DMA((heads,)),
        ],
        compiler_params=pltpu.CompilerParams(collective_id=1, has_side_effects=True),
    )(carry_map, carry_add)


def gathered(x, size, me):
    turned = [x] + [
        lax.ppermute(x, "context", [(i, (i + step) % size) for i in range(size)])
        for step in range(1, size)
    ]
    return jnp.stack(turned), (me - jnp.arange(size, dtype=jnp.int32)) % size


def unit_lower_inverse(lower):
    size = lower.shape[-1]
    index = jnp.arange(size)
    inverse = jnp.eye(size, dtype=jnp.float32)[None] - jnp.where(
        (index[:, None] // 2 == index[None, :] // 2)[None], lower, 0.0
    )
    width = 2
    while width < size:
        block = index // width
        pair = (block[:, None] // 2 == block[None, :] // 2) & (block[:, None] > block[None, :])
        cross = jnp.where(pair[None], lower, 0.0)
        half = jnp.einsum("hij,hjk->hik", cross, inverse, precision=HIGH)
        inverse = inverse - jnp.einsum("hij,hjk->hik", inverse, half, precision=HIGH)
        width *= 2
    return inverse


def yarn_tables(positions, rotary):
    half = rotary // 2
    log_theta = math.log(ROPE_THETA)
    lower = max(
        math.floor(rotary * math.log(YARN_ANCHOR / (64.0 * math.pi)) / (2.0 * log_theta)), 0
    )
    upper = min(
        math.ceil(rotary * math.log(YARN_ANCHOR / (2.0 * math.pi)) / (2.0 * log_theta)), rotary - 1
    )
    spread = float(upper - lower)
    index = jnp.arange(half, dtype=jnp.float32)
    plain_frequency = jnp.exp(index * (-2.0 * log_theta / rotary))
    keep = 1.0 - jnp.clip((index - lower) / spread, 0.0, 1.0)
    frequency = plain_frequency * keep + plain_frequency / YARN_FACTOR * (1.0 - keep)
    angles = positions.astype(jnp.float32)[:, None] * frequency[None, :]
    attention_factor = 0.1 * math.log(YARN_FACTOR) + 1.0
    return (jnp.cos(angles) * attention_factor, jnp.sin(angles) * attention_factor)


def rotate(values, cosines, sines, rotary):
    half = rotary // 2
    first = values[..., :half]
    second = values[..., half:rotary]
    cosines = cosines[:, None, :]
    sines = sines[:, None, :]
    return jnp.concatenate(
        [first * cosines - second * sines, second * cosines + first * sines, values[..., rotary:]],
        axis=-1,
    )


def unit_rows(values):
    return values * lax.rsqrt(jnp.sum(values * values, axis=-1, keepdims=True) + 1e-06)


def row_layout(rows, req_len, req_prefix, req_offset):
    starts = jnp.cumsum(req_len) - req_len
    leading_found = (starts[None, :] <= rows[:, None]).astype(jnp.int32)
    segment = jnp.sum(leading_found, axis=1) - 1
    choose = (segment[:, None] == jnp.arange(req_len.shape[0], dtype=jnp.int32)[None, :]).astype(
        jnp.int32
    )
    first = jnp.sum(choose * starts[None, :], axis=1)
    prefix = jnp.sum(choose * req_prefix[None, :], axis=1)
    offset = jnp.sum(choose * req_offset[None, :], axis=1)
    return (segment, first, prefix, offset, offset + rows - first)


def absorb(state, queries, search_handles, values, visible):
    peak, total, summed = state
    scores = jnp.einsum(
        "thd,nd->thn", queries, search_handles, preferred_element_type=jnp.float32
    ) * search_handles.shape[-1] ** (-0.5)
    seen = visible[:, None, :]
    scores = jnp.where(seen, scores, NEG_LARGE)
    new_peak = jnp.maximum(peak, jnp.max(scores, axis=-1))
    weights = jnp.where(seen, jnp.exp(scores - new_peak[..., None]), 0.0)
    shrink = jnp.exp(peak - new_peak)
    total = total * shrink + jnp.sum(weights, axis=-1)
    summed = summed * shrink[..., None] + jnp.einsum(
        "thn,nd->thd", weights.astype(jnp.bfloat16), values, preferred_element_type=jnp.float32
    )
    return (new_peak, total, summed)


def shards(
    dn_query,
    dn_key,
    dn_value,
    dn_gate,
    dn_beta_logit,
    dn_decay,
    dn_norm_gain,
    prefix_state,
    at_query,
    at_gate,
    at_key,
    at_value,
    prefix_key,
    prefix_value,
    req_len,
    req_prefix,
    req_offset,
    block_table,
):
    tokens_here = dn_query.shape[0]
    key_heads = dn_query.shape[1] // DK
    value_heads = dn_value.shape[1] // DV
    query_heads = at_query.shape[1] // HD
    device = lax.axis_index("context")
    row_start = device * tokens_here
    rows = row_start + jnp.arange(tokens_here, dtype=jnp.int32)
    segment, first, prefix, offset, position = row_layout(rows, req_len, req_prefix, req_offset)
    size = lax.axis_size("context")
    query_heads_here = query_heads
    kv_head = lax.axis_index("head") * query_heads_here // (HQ // KVH)
    cosines, sines = yarn_tables(position, ROT)
    new_key = lax.dynamic_slice_in_dim(at_key, kv_head * HD, HD, 1).reshape(tokens_here, 1, HD)
    new_key = (
        rotate(new_key.astype(jnp.float32), cosines, sines, ROT)
        .reshape(tokens_here, HD)
        .astype(jnp.bfloat16)
    )
    new_value = lax.dynamic_slice_in_dim(at_value, kv_head * HD, HD, 1)
    cached_key = lax.dynamic_slice_in_dim(prefix_key, kv_head * HD, HD, 2)
    cached_value = lax.dynamic_slice_in_dim(prefix_value, kv_head * HD, HD, 2)
    states, origin = gathered(prefix_state, size, device)
    states = jnp.take(states, origin, axis=0)
    states = jnp.moveaxis(states, 0, 2)
    states = states.reshape(states.shape[:2] + (-1, DK))
    slots_here = cached_key.shape[0]
    both, origin = gathered(
        jnp.concatenate(
            [cached_key.reshape(-1, HD), new_key, cached_value.reshape(-1, HD), new_value]
        ).reshape(2, -1, HD),
        size,
        device,
    )
    cached_rows = cached_key.shape[0] * cached_key.shape[1]
    query = jnp.repeat(
        unit_rows(dn_query.reshape(tokens_here, key_heads, DK).astype(jnp.float32)) * DK ** (-0.5),
        VH // KH,
        axis=1,
    )
    key = jnp.repeat(
        unit_rows(dn_key.reshape(tokens_here, key_heads, DK).astype(jnp.float32)), VH // KH, axis=1
    )
    query_heads_first = jnp.transpose(query, (1, 0, 2))
    key_heads_first = jnp.transpose(key, (1, 0, 2))
    value_heads_first = jnp.transpose(
        dn_value.reshape(tokens_here, value_heads, DV).astype(jnp.float32), (1, 0, 2)
    )
    beta = jax.nn.sigmoid(dn_beta_logit).T
    same = segment[:, None] == segment[None, :]
    causal = same & (rows[:, None] >= rows[None, :])
    strict = same & (rows[:, None] > rows[None, :])
    running = jnp.dot(causal.astype(jnp.float32), dn_decay, precision=HIGH).T
    gaps = running[:, :, None] - running[:, None, :]
    decay_mat = jnp.where(causal[None], jnp.exp(jnp.where(causal[None], gaps, 0.0)), 0.0)
    key_gram = jnp.einsum("hid,hjd->hij", key_heads_first, key_heads_first, precision=HIGH)
    query_key = jnp.einsum("hid,hjd->hij", query_heads_first, key_heads_first, precision=HIGH)
    lower_mat = jnp.where(strict[None], beta[:, :, None] * key_gram * decay_mat, 0.0)
    start_decay = jnp.exp(running)
    solve_values = beta[:, :, None] * value_heads_first
    solve_keys = (beta * start_decay)[:, :, None] * key_heads_first
    solved = jnp.einsum(
        "hij,hjk->hik",
        unit_lower_inverse(lower_mat),
        jnp.concatenate([solve_values, solve_keys], axis=2),
        precision=HIGH,
    )
    update = solved[:, :, :DV]
    wy_keys = solved[:, :, DV:]
    mixing = decay_mat * query_key
    local_out = jnp.einsum("hij,hjv->hiv", mixing, update, precision=HIGH)
    reach = start_decay[:, :, None] * query_heads_first - jnp.einsum(
        "hij,hjk->hik", mixing, wy_keys, precision=HIGH
    )
    tail = segment == segment[tokens_here - 1]
    end_gaps = running[:, tokens_here - 1 : tokens_here] - running
    end_weight = jnp.where(tail[None, :], jnp.exp(jnp.where(tail[None, :], end_gaps, 0.0)), 0.0)
    end_decay = start_decay[:, tokens_here - 1]
    identity_mat = jnp.eye(DK, dtype=jnp.float32)
    carry_map = end_decay[:, None, None] * identity_mat[None] - jnp.einsum(
        "hjk,hj,hjl->hkl", wy_keys, end_weight, key_heads_first, precision=HIGH
    )
    carry_add = jnp.einsum("hjv,hj,hjl->hvl", update, end_weight, key_heads_first, precision=HIGH)
    restarts = first[tokens_here - 1] >= row_start
    tail_prefix = prefix[tokens_here - 1]
    base = jnp.zeros(states.shape[1:], states.dtype)
    for owner in range(states.shape[0]):
        base = jnp.where(tail_prefix == owner, states[owner], base)
    map_half = carry_map.astype(jnp.bfloat16)
    fresh = jnp.einsum("hvj,hjk->hvk", base, map_half, preferred_element_type=jnp.float32)
    into_state = chain(
        jnp.where(restarts, 0, map_half).astype(jnp.bfloat16),
        carry_add + jnp.where(restarts, fresh, 0.0),
        size,
    )
    carried = (segment == segment[0]) & (first[0] < row_start)
    owner_ids = jnp.arange(states.shape[0], dtype=jnp.int32)
    select = (prefix[None, :] == owner_ids[:, None]) & ~carried[None, :]
    select = jnp.concatenate([select, carried[None, :]], axis=0)
    weight_vec = reach.astype(jnp.bfloat16)
    core = local_out
    for owner in range(states.shape[0] + 1):
        held = states[owner] if owner < states.shape[0] else into_state
        core = core + jnp.einsum(
            "hik,hvk->hiv",
            jnp.where(select[owner][None, :, None], weight_vec, 0),
            held,
            preferred_element_type=jnp.float32,
        )
    core_rows = jnp.transpose(core, (1, 0, 2))
    normed = core_rows * lax.rsqrt(jnp.mean(core_rows * core_rows, axis=-1, keepdims=True) + 1e-06)
    gate_rows = dn_gate.reshape(tokens_here, value_heads, DV).astype(jnp.float32)
    dn_out = (
        (normed * dn_norm_gain * jax.nn.silu(gate_rows))
        .reshape(tokens_here, value_heads * DV)
        .astype(jnp.bfloat16)
    )
    query_rot = rotate(
        at_query.reshape(tokens_here, query_heads, HD).astype(jnp.float32), cosines, sines, ROT
    ).astype(jnp.bfloat16)
    table_index = jnp.arange(block_table.shape[0], dtype=jnp.int32)
    blocks_per_prefix = block_table.shape[0] // prefix_state.shape[0]
    state = (
        jnp.full((tokens_here, query_heads), NEG_LARGE, jnp.float32),
        jnp.zeros((tokens_here, query_heads), jnp.float32),
        jnp.zeros((tokens_here, query_heads, HD), jnp.float32),
    )
    part = jnp.arange(cached_rows, dtype=jnp.int32)
    width = cached_key.shape[1]
    slots = (origin[:, None] * slots_here + part[None, :] // width).reshape(-1)
    entry = jnp.sum(
        jnp.where(block_table[None, :] == slots[:, None], table_index[None, :], 0), axis=1
    ).reshape(size, cached_rows)
    owner = entry // blocks_per_prefix
    where_in = entry % blocks_per_prefix * width + part[None, :] % width
    key_rows = origin[:, None] * tokens_here + jnp.arange(tokens_here, dtype=jnp.int32)[None, :]
    key_segment = row_layout(key_rows.reshape(-1), req_len, req_prefix, req_offset)[0]
    key_segment = key_segment.reshape(size, tokens_here)
    old_seen = (owner[None] == prefix[:, None, None]) & (where_in[None] < offset[:, None, None])
    new_seen = (key_segment[None] == segment[:, None, None]) & (key_rows[None] <= rows[:, None, None])
    visible = jnp.concatenate([old_seen, new_seen], axis=2).reshape(tokens_here, -1)
    state = absorb(
        state, query_rot, both[:, 0].reshape(-1, HD), both[:, 1].reshape(-1, HD), visible
    )
    peak, total, summed = state
    attention = summed / total[..., None]
    gate_att = at_gate.reshape(tokens_here, query_heads, HD).astype(jnp.float32)
    at_out = (
        (attention * jax.nn.sigmoid(gate_att))
        .reshape(tokens_here, query_heads * HD)
        .astype(jnp.bfloat16)
    )
    return (dn_out, at_out)


def solution(mesh):
    placed = (
        P(("group", "context"), "head"),
        P(("group", "context"), "head"),
        P(("group", "context"), "head"),
        P(("group", "context"), "head"),
        P(("group", "context"), "head"),
        P(("group", "context"), "head"),
        P(),
        P("group", "head", "context", None),
        P(("group", "context"), "head"),
        P(("group", "context"), "head"),
        P(("group", "context"), None),
        P(("group", "context"), None),
        P(("group", "context"), None, None),
        P(("group", "context"), None, None),
        P("group"),
        P("group"),
        P("group"),
        P("group"),
    )
    return jax.shard_map(
        shards,
        mesh=mesh,
        in_specs=placed,
        out_specs=(P(("group", "context"), "head"), P(("group", "context"), "head")),
        check_vma=False,
    )
```

```python
import math

import jax
import jax.numpy as jnp
from jax import lax
from jax.experimental import pallas as pl
from jax.experimental.pallas import tpu as pltpu
from jax.sharding import PartitionSpec as P

VH = 32
KH = 16
DK = 128
DV = 128
HQ = 16
KVH = 2
HD = 256
ROT = 64


ROPE_THETA = 10000000.0
YARN_FACTOR = 4.0
YARN_ANCHOR = 262144.0
NEG_LARGE = -1e30
HIGH = lax.Precision.HIGHEST


def chain_kernel(size, map_ref, add_ref, into_ref, held, leaving, send_sem, recv_sem):
    me = lax.axis_index("context")
    heads = map_ref.shape[0]
    barrier = pltpu.get_barrier_semaphore()
    after, before = lax.rem(me + 1, size), lax.rem(me + size - 1, size)
    for neighbour in (before, after):
        pl.semaphore_signal(barrier, inc=1, device_id={"context": neighbour})
    pl.semaphore_wait(barrier, 2)

    def sent(h):
        return pltpu.make_async_remote_copy(
            src_ref=leaving.at[h],
            dst_ref=held.at[h],
            send_sem=send_sem.at[h],
            recv_sem=recv_sem.at[h],
            device_id={"context": after},
        )

    @pl.when(me == 0)
    def _():
        held[...] = jnp.zeros_like(held)

    for h in range(heads):

        @pl.when(me > 0)
        def _(h=h):
            sent(h).wait_recv()

        leaving[h] = (
            jnp.dot(held[h], map_ref[h], preferred_element_type=jnp.float32) + add_ref[h]
        ).astype(jnp.bfloat16)

        @pl.when(me < size - 1)
        def _(h=h):
            sent(h).start()

    into_ref[...] = held[...]

    @pl.when(me < size - 1)
    def _():
        for h in range(heads):
            sent(h).wait_send()


def chain(carry_map, carry_add, size):
    heads = carry_map.shape[0]
    return pl.pallas_call(
        lambda *refs: chain_kernel(size, *refs),
        out_shape=jax.ShapeDtypeStruct(carry_add.shape, jnp.bfloat16),
        in_specs=[pl.BlockSpec(memory_space=pltpu.VMEM)] * 2,
        out_specs=pl.BlockSpec(memory_space=pltpu.VMEM),
        scratch_shapes=[
            pltpu.VMEM(carry_add.shape, jnp.bfloat16),
            pltpu.VMEM(carry_add.shape, jnp.bfloat16),
            pltpu.SemaphoreType.DMA((heads,)),
            pltpu.SemaphoreType.DMA((heads,)),
        ],
        compiler_params=pltpu.CompilerParams(collective_id=1, has_side_effects=True),
    )(carry_map, carry_add)


def gathered(x, size, me):
    turned = [x] + [
        lax.ppermute(x, "context", [(i, (i + step) % size) for i in range(size)])
        for step in range(1, size)
    ]
    return jnp.stack(turned), (me - jnp.arange(size, dtype=jnp.int32)) % size


def halves(x):
    high = x.astype(jnp.bfloat16)
    return high, (x - high.astype(jnp.float32)).astype(jnp.bfloat16)


def dot1(a, b, contract=((1,), (0,))):
    return lax.dot_general(a, b, (contract, ((), ())), preferred_element_type=jnp.float32)


def dot2(a, exact):
    high, low = halves(a)
    return dot1(high, exact) + dot1(low, exact)


def dot3(a, b):
    a_high, a_low = halves(a)
    b_high, b_low = halves(b)
    return dot1(a_high, b_high) + (dot1(a_high, b_low) + dot1(a_low, b_high))


def local_kernel(
    query_ref, key_ref, value_ref, logit_ref, logit_row_ref, decay_ref, decay_row_ref,
    seg_ref, seg_row_ref, local_ref, reach_ref, map_ref, add_ref,
):
    tokens = query_ref.shape[0]
    heads = local_ref.shape[0]
    share = VH // KH
    seg, seg_row = seg_ref[...], seg_row_ref[...]
    row = lax.broadcasted_iota(jnp.int32, (tokens, tokens), 0)
    col = lax.broadcasted_iota(jnp.int32, (tokens, tokens), 1)
    same = seg == seg_row
    causal = same & (row >= col)
    strict = same & (row > col)
    eye = row == col
    causal_f = causal.astype(jnp.float32)
    run = lax.dot_general(
        causal_f, decay_ref[...], (((1,), (0,)), ((), ())),
        precision=HIGH, preferred_element_type=jnp.float32,
    )
    run_row = lax.dot_general(
        decay_row_ref[...], causal_f, (((1,), (1,)), ((), ())),
        precision=HIGH, preferred_element_type=jnp.float32,
    )
    beta, beta_row = jax.nn.sigmoid(logit_ref[...]), jax.nn.sigmoid(logit_row_ref[...])
    start, start_row = jnp.exp(run), jnp.exp(run_row)
    tail = seg_row == seg_row[:, tokens - 1 : tokens]
    end_row = jnp.where(
        tail, jnp.exp(jnp.where(tail, run_row[:, tokens - 1 : tokens] - run_row, 0.0)), 0.0
    )
    keys, grams, mixes, scaled, inv_rows = [], [], [], [], []
    for g in range(heads // share):
        k = key_ref[:, g * DK : (g + 1) * DK]
        q = query_ref[:, g * DK : (g + 1) * DK]
        gram = dot1(k, k, ((1,), (1,)))
        cross = dot1(q, k, ((1,), (1,)))
        squares = jnp.where(eye, gram, 0.0)
        inv = lax.rsqrt(jnp.sum(squares, axis=1, keepdims=True) + 1e-06)
        inv_row = lax.rsqrt(jnp.sum(squares, axis=0, keepdims=True) + 1e-06)
        q_f = q.astype(jnp.float32)
        inv_q = lax.rsqrt(jnp.sum(q_f * q_f, axis=1, keepdims=True) + 1e-06) * DK ** (-0.5)
        keys.append(k)
        inv_rows.append(inv_row)
        grams.append(gram * inv * inv_row)
        mixes.append(cross * inv_q * inv_row)
        scaled.append(q_f * inv_q)
    lowers, inverses, mixing = [], [], []
    for h in range(heads):
        gaps = run[:, h : h + 1] - run_row[h : h + 1, :]
        decay_mat = jnp.where(causal, jnp.exp(jnp.where(causal, gaps, 0.0)), 0.0)
        mixing.append(decay_mat * mixes[h // share])
        lower = jnp.where(strict, beta[:, h : h + 1] * grams[h // share] * decay_mat, 0.0)
        lowers.append(lower)
        inverses.append(
            jnp.where(eye, 1.0, 0.0) - jnp.where(row // 2 == col // 2, lower, 0.0)
        )
    width = 2
    while width < tokens:
        pair = (row // (2 * width) == col // (2 * width)) & (row // width > col // width)
        half = [dot3(jnp.where(pair, lowers[h], 0.0), inverses[h]) for h in range(heads)]
        inverses = [inverses[h] - dot3(inverses[h], half[h]) for h in range(heads)]
        width *= 2
    for h in range(heads):
        g = h // share
        weighted = inverses[h] * beta_row[h : h + 1, :]
        update = dot2(weighted, value_ref[:, h * DV : (h + 1) * DV])
        wy = dot2(weighted * (start_row[h : h + 1, :] * inv_rows[g]), keys[g])
        solved = jnp.concatenate([update, wy], axis=1)
        mixed = dot3(mixing[h], solved)
        local_ref[h] = mixed[:, :DV]
        reach_ref[h] = (start[:, h : h + 1] * scaled[g] - mixed[:, DV:]).astype(jnp.bfloat16)
        turned = solved.T * (end_row[h : h + 1, :] * inv_rows[g])
        carry = dot2(turned, keys[g])
        add_ref[h] = carry[:DV]
        map_ref[h] = (
            jnp.where(eye, start[tokens - 1 : tokens, h : h + 1], 0.0) - carry[DV:]
        ).astype(jnp.bfloat16)


def finish_kernel(local_ref, reach_ref, states_ref, into_ref, select_ref, gate_ref, gain_ref, out_ref):
    owners = states_ref.shape[0]
    select = select_ref[...] > 0.5
    for h in range(local_ref.shape[0]):
        core = local_ref[h]
        reach = reach_ref[h]
        for owner in range(owners + 1):
            state = states_ref[owner, h] if owner < owners else into_ref[h]
            part = dot1(reach, state, ((1,), (1,)))
            core = core + jnp.where(select[:, owner : owner + 1], part, 0.0)
        normed = core * lax.rsqrt(jnp.mean(core * core, axis=1, keepdims=True) + 1e-06)
        gate = gate_ref[:, h * DV : (h + 1) * DV].astype(jnp.float32)
        out_ref[:, h * DV : (h + 1) * DV] = (
            normed * gain_ref[...] * (gate * jax.nn.sigmoid(gate))
        ).astype(jnp.bfloat16)


def whole_call(kernel, shapes, *arrays):
    space = pl.BlockSpec(memory_space=pltpu.VMEM)
    return pl.pallas_call(
        kernel,
        out_shape=shapes,
        in_specs=[space] * len(arrays),
        out_specs=jax.tree.map(lambda _: space, shapes),
        compiler_params=pltpu.CompilerParams(vmem_limit_bytes=48 * 2**20),
    )(*arrays)


def yarn_tables(positions, rotary):
    half = rotary // 2
    log_theta = math.log(ROPE_THETA)
    lower = max(
        math.floor(rotary * math.log(YARN_ANCHOR / (64.0 * math.pi)) / (2.0 * log_theta)), 0
    )
    upper = min(
        math.ceil(rotary * math.log(YARN_ANCHOR / (2.0 * math.pi)) / (2.0 * log_theta)), rotary - 1
    )
    spread = float(upper - lower)
    index = jnp.arange(half, dtype=jnp.float32)
    plain_frequency = jnp.exp(index * (-2.0 * log_theta / rotary))
    keep = 1.0 - jnp.clip((index - lower) / spread, 0.0, 1.0)
    frequency = plain_frequency * keep + plain_frequency / YARN_FACTOR * (1.0 - keep)
    angles = positions.astype(jnp.float32)[:, None] * frequency[None, :]
    attention_factor = 0.1 * math.log(YARN_FACTOR) + 1.0
    return (jnp.cos(angles) * attention_factor, jnp.sin(angles) * attention_factor)


def rotate(values, cosines, sines, rotary):
    half = rotary // 2
    first = values[..., :half]
    second = values[..., half:rotary]
    cosines = cosines[:, None, :]
    sines = sines[:, None, :]
    return jnp.concatenate(
        [first * cosines - second * sines, second * cosines + first * sines, values[..., rotary:]],
        axis=-1,
    )


def row_layout(rows, req_len, req_prefix, req_offset):
    starts = jnp.cumsum(req_len) - req_len
    leading_found = (starts[None, :] <= rows[:, None]).astype(jnp.int32)
    segment = jnp.sum(leading_found, axis=1) - 1
    choose = (segment[:, None] == jnp.arange(req_len.shape[0], dtype=jnp.int32)[None, :]).astype(
        jnp.int32
    )
    first = jnp.sum(choose * starts[None, :], axis=1)
    prefix = jnp.sum(choose * req_prefix[None, :], axis=1)
    offset = jnp.sum(choose * req_offset[None, :], axis=1)
    return (segment, first, prefix, offset, offset + rows - first)


def absorb(state, queries, search_handles, values, visible):
    peak, total, summed = state
    scores = jnp.einsum(
        "thd,nd->thn", queries, search_handles, preferred_element_type=jnp.float32
    ) * search_handles.shape[-1] ** (-0.5)
    seen = visible[:, None, :]
    scores = jnp.where(seen, scores, NEG_LARGE)
    new_peak = jnp.maximum(peak, jnp.max(scores, axis=-1))
    weights = jnp.where(seen, jnp.exp(scores - new_peak[..., None]), 0.0)
    shrink = jnp.exp(peak - new_peak)
    total = total * shrink + jnp.sum(weights, axis=-1)
    summed = summed * shrink[..., None] + jnp.einsum(
        "thn,nd->thd", weights.astype(jnp.bfloat16), values, preferred_element_type=jnp.float32
    )
    return (new_peak, total, summed)


def shards(
    dn_query,
    dn_key,
    dn_value,
    dn_gate,
    dn_beta_logit,
    dn_decay,
    dn_norm_gain,
    prefix_state,
    at_query,
    at_gate,
    at_key,
    at_value,
    prefix_key,
    prefix_value,
    req_len,
    req_prefix,
    req_offset,
    block_table,
):
    tokens_here = dn_query.shape[0]
    value_heads = dn_value.shape[1] // DV
    query_heads = at_query.shape[1] // HD
    device = lax.axis_index("context")
    row_start = device * tokens_here
    rows = row_start + jnp.arange(tokens_here, dtype=jnp.int32)
    segment, first, prefix, offset, position = row_layout(rows, req_len, req_prefix, req_offset)
    size = lax.axis_size("context")
    query_heads_here = query_heads
    kv_head = lax.axis_index("head") * query_heads_here // (HQ // KVH)
    cosines, sines = yarn_tables(position, ROT)
    new_key = lax.dynamic_slice_in_dim(at_key, kv_head * HD, HD, 1).reshape(tokens_here, 1, HD)
    new_key = (
        rotate(new_key.astype(jnp.float32), cosines, sines, ROT)
        .reshape(tokens_here, HD)
        .astype(jnp.bfloat16)
    )
    new_value = lax.dynamic_slice_in_dim(at_value, kv_head * HD, HD, 1)
    cached_key = lax.dynamic_slice_in_dim(prefix_key, kv_head * HD, HD, 2)
    cached_value = lax.dynamic_slice_in_dim(prefix_value, kv_head * HD, HD, 2)
    states, origin = gathered(prefix_state, size, device)
    states = jnp.take(states, origin, axis=0)
    states = jnp.moveaxis(states, 0, 2)
    states = states.reshape(states.shape[:2] + (-1, DK))
    slots_here = cached_key.shape[0]
    both, origin = gathered(
        jnp.concatenate(
            [cached_key.reshape(-1, HD), new_key, cached_value.reshape(-1, HD), new_value]
        ).reshape(2, -1, HD),
        size,
        device,
    )
    cached_rows = cached_key.shape[0] * cached_key.shape[1]
    square = (value_heads, DK, DK)
    local_out, reach, map_half, carry_add = whole_call(
        local_kernel,
        [
            jax.ShapeDtypeStruct((value_heads, tokens_here, DV), jnp.float32),
            jax.ShapeDtypeStruct((value_heads, tokens_here, DK), jnp.bfloat16),
            jax.ShapeDtypeStruct(square, jnp.bfloat16),
            jax.ShapeDtypeStruct(square, jnp.float32),
        ],
        dn_query,
        dn_key,
        dn_value,
        dn_beta_logit,
        dn_beta_logit.T,
        dn_decay,
        dn_decay.T,
        segment[:, None],
        segment[None, :],
    )
    restarts = first[tokens_here - 1] >= row_start
    tail_prefix = prefix[tokens_here - 1]
    base = jnp.zeros(states.shape[1:], states.dtype)
    for owner in range(states.shape[0]):
        base = jnp.where(tail_prefix == owner, states[owner], base)
    fresh = jnp.einsum("hvj,hjk->hvk", base, map_half, preferred_element_type=jnp.float32)
    into_state = chain(
        jnp.where(restarts, 0, map_half).astype(jnp.bfloat16),
        carry_add + jnp.where(restarts, fresh, 0.0),
        size,
    )
    carried = (segment == segment[0]) & (first[0] < row_start)
    owner_ids = jnp.arange(states.shape[0], dtype=jnp.int32)
    select = (prefix[None, :] == owner_ids[:, None]) & ~carried[None, :]
    select = jnp.concatenate([select, carried[None, :]], axis=0)
    dn_out = whole_call(
        finish_kernel,
        jax.ShapeDtypeStruct((tokens_here, value_heads * DV), jnp.bfloat16),
        local_out,
        reach,
        states,
        into_state,
        select.astype(jnp.float32).T,
        dn_gate,
        dn_norm_gain[None, :],
    )
    query_rot = rotate(
        at_query.reshape(tokens_here, query_heads, HD).astype(jnp.float32), cosines, sines, ROT
    ).astype(jnp.bfloat16)
    table_index = jnp.arange(block_table.shape[0], dtype=jnp.int32)
    blocks_per_prefix = block_table.shape[0] // prefix_state.shape[0]
    state = (
        jnp.full((tokens_here, query_heads), NEG_LARGE, jnp.float32),
        jnp.zeros((tokens_here, query_heads), jnp.float32),
        jnp.zeros((tokens_here, query_heads, HD), jnp.float32),
    )
    part = jnp.arange(cached_rows, dtype=jnp.int32)
    width = cached_key.shape[1]
    slots = (origin[:, None] * slots_here + part[None, :] // width).reshape(-1)
    entry = jnp.sum(
        jnp.where(block_table[None, :] == slots[:, None], table_index[None, :], 0), axis=1
    ).reshape(size, cached_rows)
    owner = entry // blocks_per_prefix
    where_in = entry % blocks_per_prefix * width + part[None, :] % width
    key_rows = origin[:, None] * tokens_here + jnp.arange(tokens_here, dtype=jnp.int32)[None, :]
    key_segment = row_layout(key_rows.reshape(-1), req_len, req_prefix, req_offset)[0]
    key_segment = key_segment.reshape(size, tokens_here)
    old_seen = (owner[None] == prefix[:, None, None]) & (where_in[None] < offset[:, None, None])
    new_seen = (key_segment[None] == segment[:, None, None]) & (key_rows[None] <= rows[:, None, None])
    visible = jnp.concatenate([old_seen, new_seen], axis=2).reshape(tokens_here, -1)
    state = absorb(
        state, query_rot, both[:, 0].reshape(-1, HD), both[:, 1].reshape(-1, HD), visible
    )
    peak, total, summed = state
    attention = summed / total[..., None]
    gate_att = at_gate.reshape(tokens_here, query_heads, HD).astype(jnp.float32)
    at_out = (
        (attention * jax.nn.sigmoid(gate_att))
        .reshape(tokens_here, query_heads * HD)
        .astype(jnp.bfloat16)
    )
    return (dn_out, at_out)


def solution(mesh):
    placed = (
        P(("group", "context"), "head"),
        P(("group", "context"), "head"),
        P(("group", "context"), "head"),
        P(("group", "context"), "head"),
        P(("group", "context"), "head"),
        P(("group", "context"), "head"),
        P(),
        P("group", "head", "context", None),
        P(("group", "context"), "head"),
        P(("group", "context"), "head"),
        P(("group", "context"), None),
        P(("group", "context"), None),
        P(("group", "context"), None, None),
        P(("group", "context"), None, None),
        P("group"),
        P("group"),
        P("group"),
        P("group"),
    )
    return jax.shard_map(
        shards,
        mesh=mesh,
        in_specs=placed,
        out_specs=(P(("group", "context"), "head"), P(("group", "context"), "head")),
        check_vma=False,
    )
```

```python
import math

import jax
import jax.numpy as jnp
from jax import lax
from jax.experimental import pallas as pl
from jax.experimental.pallas import tpu as pltpu
from jax.sharding import PartitionSpec as P

VH = 32
KH = 16
DK = 128
DV = 128
HQ = 16
KVH = 2
HD = 256
ROT = 64


ROPE_THETA = 10000000.0
YARN_FACTOR = 4.0
YARN_ANCHOR = 262144.0
NEG_LARGE = -1e30
HIGH = lax.Precision.HIGHEST


def chain_kernel(size, map_ref, add_ref, into_ref, held, leaving, send_sem, recv_sem):
    me = lax.axis_index("context")
    heads = map_ref.shape[0]
    barrier = pltpu.get_barrier_semaphore()
    after, before = lax.rem(me + 1, size), lax.rem(me + size - 1, size)
    for neighbour in (before, after):
        pl.semaphore_signal(barrier, inc=1, device_id={"context": neighbour})
    pl.semaphore_wait(barrier, 2)

    def sent(h):
        return pltpu.make_async_remote_copy(
            src_ref=leaving.at[h],
            dst_ref=held.at[h],
            send_sem=send_sem.at[h],
            recv_sem=recv_sem.at[h],
            device_id={"context": after},
        )

    @pl.when(me == 0)
    def _():
        held[...] = jnp.zeros_like(held)

    for h in range(heads):

        @pl.when(me > 0)
        def _(h=h):
            sent(h).wait_recv()

        leaving[h] = (
            jnp.dot(held[h], map_ref[h], preferred_element_type=jnp.float32) + add_ref[h]
        ).astype(jnp.bfloat16)

        @pl.when(me < size - 1)
        def _(h=h):
            sent(h).start()

    into_ref[...] = held[...]

    @pl.when(me < size - 1)
    def _():
        for h in range(heads):
            sent(h).wait_send()


def chain(carry_map, carry_add, size):
    heads = carry_map.shape[0]
    return pl.pallas_call(
        lambda *refs: chain_kernel(size, *refs),
        out_shape=jax.ShapeDtypeStruct(carry_add.shape, jnp.bfloat16),
        in_specs=[pl.BlockSpec(memory_space=pltpu.VMEM)] * 2,
        out_specs=pl.BlockSpec(memory_space=pltpu.VMEM),
        scratch_shapes=[
            pltpu.VMEM(carry_add.shape, jnp.bfloat16),
            pltpu.VMEM(carry_add.shape, jnp.bfloat16),
            pltpu.SemaphoreType.DMA((heads,)),
            pltpu.SemaphoreType.DMA((heads,)),
        ],
        compiler_params=pltpu.CompilerParams(collective_id=1, has_side_effects=True),
    )(carry_map, carry_add)


def from_others(x, axis, size, span):
    return [
        lax.ppermute(
            x, axis, [(i, i // span * span + (i + step) % span) for i in range(size)]
        )
        for step in range(1, span)
    ]


def halves(x):
    high = x.astype(jnp.bfloat16)
    return high, (x - high.astype(jnp.float32)).astype(jnp.bfloat16)


def dot1(a, b, contract=((1,), (0,))):
    return lax.dot_general(a, b, (contract, ((), ())), preferred_element_type=jnp.float32)


def dot2(a, exact):
    high, low = halves(a)
    return dot1(high, exact) + dot1(low, exact)


def dot3(a, b):
    a_high, a_low = halves(a)
    b_high, b_low = halves(b)
    return dot1(a_high, b_high) + (dot1(a_high, b_low) + dot1(a_low, b_high))


def local_kernel(
    query_ref, key_ref, value_ref, logit_ref, logit_row_ref, decay_ref, decay_row_ref,
    seg_ref, seg_row_ref, local_ref, reach_ref, map_ref, add_ref,
):
    tokens = query_ref.shape[0]
    heads = local_ref.shape[0]
    share = VH // KH
    seg, seg_row = seg_ref[...], seg_row_ref[...]
    row = lax.broadcasted_iota(jnp.int32, (tokens, tokens), 0)
    col = lax.broadcasted_iota(jnp.int32, (tokens, tokens), 1)
    same = seg == seg_row
    causal = same & (row >= col)
    strict = same & (row > col)
    eye = row == col
    causal_f = causal.astype(jnp.float32)
    run = lax.dot_general(
        causal_f, decay_ref[...], (((1,), (0,)), ((), ())),
        precision=HIGH, preferred_element_type=jnp.float32,
    )
    run_row = lax.dot_general(
        decay_row_ref[...], causal_f, (((1,), (1,)), ((), ())),
        precision=HIGH, preferred_element_type=jnp.float32,
    )
    beta, beta_row = jax.nn.sigmoid(logit_ref[...]), jax.nn.sigmoid(logit_row_ref[...])
    start, start_row = jnp.exp(run), jnp.exp(run_row)
    tail = seg_row == seg_row[:, tokens - 1 : tokens]
    end_row = jnp.where(
        tail, jnp.exp(jnp.where(tail, run_row[:, tokens - 1 : tokens] - run_row, 0.0)), 0.0
    )
    keys, grams, mixes, scaled, inv_rows = [], [], [], [], []
    for g in range(heads // share):
        k = key_ref[:, g * DK : (g + 1) * DK]
        q = query_ref[:, g * DK : (g + 1) * DK]
        gram = dot1(k, k, ((1,), (1,)))
        cross = dot1(q, k, ((1,), (1,)))
        squares = jnp.where(eye, gram, 0.0)
        inv = lax.rsqrt(jnp.sum(squares, axis=1, keepdims=True) + 1e-06)
        inv_row = lax.rsqrt(jnp.sum(squares, axis=0, keepdims=True) + 1e-06)
        q_f = q.astype(jnp.float32)
        inv_q = lax.rsqrt(jnp.sum(q_f * q_f, axis=1, keepdims=True) + 1e-06) * DK ** (-0.5)
        keys.append(k)
        inv_rows.append(inv_row)
        grams.append(gram * inv * inv_row)
        mixes.append(cross * inv_q * inv_row)
        scaled.append(q_f * inv_q)
    lowers, inverses, mixing = [], [], []
    for h in range(heads):
        gaps = run[:, h : h + 1] - run_row[h : h + 1, :]
        decay_mat = jnp.where(causal, jnp.exp(jnp.where(causal, gaps, 0.0)), 0.0)
        mixing.append(decay_mat * mixes[h // share])
        lower = jnp.where(strict, beta[:, h : h + 1] * grams[h // share] * decay_mat, 0.0)
        lowers.append(lower)
        inverses.append(
            jnp.where(eye, 1.0, 0.0) - jnp.where(row // 2 == col // 2, lower, 0.0)
        )
    width = 2
    while width < tokens:
        pair = (row // (2 * width) == col // (2 * width)) & (row // width > col // width)
        half = [dot3(jnp.where(pair, lowers[h], 0.0), inverses[h]) for h in range(heads)]
        inverses = [inverses[h] - dot3(inverses[h], half[h]) for h in range(heads)]
        width *= 2
    for h in range(heads):
        g = h // share
        weighted = inverses[h] * beta_row[h : h + 1, :]
        update = dot2(weighted, value_ref[:, h * DV : (h + 1) * DV])
        wy = dot2(weighted * (start_row[h : h + 1, :] * inv_rows[g]), keys[g])
        solved = jnp.concatenate([update, wy], axis=1)
        mixed = dot3(mixing[h], solved)
        local_ref[h] = mixed[:, :DV]
        reach_ref[h] = (start[:, h : h + 1] * scaled[g] - mixed[:, DV:]).astype(jnp.bfloat16)
        turned = solved.T * (end_row[h : h + 1, :] * inv_rows[g])
        carry = dot2(turned, keys[g])
        add_ref[h] = carry[:DV]
        map_ref[h] = (
            jnp.where(eye, start[tokens - 1 : tokens, h : h + 1], 0.0) - carry[DV:]
        ).astype(jnp.bfloat16)


def finish_kernel(local_ref, reach_ref, states_ref, into_ref, select_ref, gate_ref, gain_ref, out_ref):
    owners = states_ref.shape[0]
    select = select_ref[...] > 0.5
    for h in range(local_ref.shape[0]):
        core = local_ref[h]
        reach = reach_ref[h]
        for owner in range(owners + 1):
            state = states_ref[owner, h] if owner < owners else into_ref[h]
            part = dot1(reach, state, ((1,), (1,)))
            core = core + jnp.where(select[:, owner : owner + 1], part, 0.0)
        normed = core * lax.rsqrt(jnp.mean(core * core, axis=1, keepdims=True) + 1e-06)
        gate = gate_ref[:, h * DV : (h + 1) * DV].astype(jnp.float32)
        out_ref[:, h * DV : (h + 1) * DV] = (
            normed * gain_ref[...] * (gate * jax.nn.sigmoid(gate))
        ).astype(jnp.bfloat16)


def attend_kernel(
    query_ref, cos_ref, sin_ref, gate_ref, row_ref, code_ref, place_ref, own_ref, *rest
):
    pieces, out_ref = [own_ref] + list(rest[:-1]), rest[-1]
    tokens = query_ref.shape[0]
    cosines, sines = cos_ref[...], sin_ref[...]
    lane = lax.broadcasted_iota(jnp.int32, (tokens, 128), 1)
    old_code, limit = row_ref[:, 0:1], row_ref[:, 1:2]
    new_code, own_row = row_ref[:, 2:3], row_ref[:, 3:4]
    keys, values, seen, at = [], [], [], 0
    for ref in pieces:
        if len(ref.shape) == 3:
            keys.append(ref[0])
            values.append(ref[1])
        else:
            keys.append(ref[:, 0].reshape(-1, HD))
            values.append(ref[:, 1].reshape(-1, HD))
        count = keys[-1].shape[0]
        code, place = code_ref[:, at : at + count], place_ref[:, at : at + count]
        at += count
        seen.append(
            ((code == old_code) & (place < limit)) | ((code == new_code) & (place <= own_row))
        )
    for h in range(query_ref.shape[1] // HD):
        front = query_ref[:, h * HD : h * HD + 128].astype(jnp.float32)
        swapped = jnp.where(
            lane < ROT // 2, pltpu.roll(front, 128 - ROT // 2, 1), pltpu.roll(front, ROT // 2, 1)
        )
        query = jnp.concatenate(
            [
                (front * cosines + swapped * sines).astype(jnp.bfloat16),
                query_ref[:, h * HD + 128 : (h + 1) * HD],
            ],
            axis=1,
        )
        scores = [
            jnp.where(see, dot1(query, key, ((1,), (1,))) * HD ** (-0.5), NEG_LARGE)
            for see, key in zip(seen, keys)
        ]
        peak = jnp.max(scores[0], axis=1, keepdims=True)
        for score in scores[1:]:
            peak = jnp.maximum(peak, jnp.max(score, axis=1, keepdims=True))
        total, summed = 0.0, 0.0
        for score, see, value in zip(scores, seen, values):
            weight = jnp.where(see, jnp.exp(score - peak), 0.0)
            total = total + jnp.sum(weight, axis=1, keepdims=True)
            summed = summed + dot1(weight.astype(jnp.bfloat16), value)
        gate = gate_ref[:, h * HD : (h + 1) * HD].astype(jnp.float32)
        out_ref[:, h * HD : (h + 1) * HD] = (
            summed / total * jax.nn.sigmoid(gate)
        ).astype(jnp.bfloat16)


def whole_call(kernel, shapes, *arrays):
    space = pl.BlockSpec(memory_space=pltpu.VMEM)
    return pl.pallas_call(
        kernel,
        out_shape=shapes,
        in_specs=[space] * len(arrays),
        out_specs=jax.tree.map(lambda _: space, shapes),
        compiler_params=pltpu.CompilerParams(vmem_limit_bytes=48 * 2**20),
    )(*arrays)


def yarn_tables(positions, rotary):
    half = rotary // 2
    log_theta = math.log(ROPE_THETA)
    lower = max(
        math.floor(rotary * math.log(YARN_ANCHOR / (64.0 * math.pi)) / (2.0 * log_theta)), 0
    )
    upper = min(
        math.ceil(rotary * math.log(YARN_ANCHOR / (2.0 * math.pi)) / (2.0 * log_theta)), rotary - 1
    )
    spread = float(upper - lower)
    index = jnp.arange(half, dtype=jnp.float32)
    plain_frequency = jnp.exp(index * (-2.0 * log_theta / rotary))
    keep = 1.0 - jnp.clip((index - lower) / spread, 0.0, 1.0)
    frequency = plain_frequency * keep + plain_frequency / YARN_FACTOR * (1.0 - keep)
    angles = positions.astype(jnp.float32)[:, None] * frequency[None, :]
    attention_factor = 0.1 * math.log(YARN_FACTOR) + 1.0
    return (jnp.cos(angles) * attention_factor, jnp.sin(angles) * attention_factor)


def rotate(values, cosines, sines, rotary):
    half = rotary // 2
    first = values[..., :half]
    second = values[..., half:rotary]
    cosines = cosines[:, None, :]
    sines = sines[:, None, :]
    return jnp.concatenate(
        [first * cosines - second * sines, second * cosines + first * sines, values[..., rotary:]],
        axis=-1,
    )


def row_layout(rows, req_len, req_prefix, req_offset):
    starts = jnp.cumsum(req_len) - req_len
    leading_found = (starts[None, :] <= rows[:, None]).astype(jnp.int32)
    segment = jnp.sum(leading_found, axis=1) - 1
    choose = (segment[:, None] == jnp.arange(req_len.shape[0], dtype=jnp.int32)[None, :]).astype(
        jnp.int32
    )
    first = jnp.sum(choose * starts[None, :], axis=1)
    prefix = jnp.sum(choose * req_prefix[None, :], axis=1)
    offset = jnp.sum(choose * req_offset[None, :], axis=1)
    return (segment, first, prefix, offset, offset + rows - first)


def shards(
    dn_query,
    dn_key,
    dn_value,
    dn_gate,
    dn_beta_logit,
    dn_decay,
    dn_norm_gain,
    prefix_state,
    at_query,
    at_gate,
    at_key,
    at_value,
    prefix_key,
    prefix_value,
    req_len,
    req_prefix,
    req_offset,
    block_table,
):
    tokens_here = dn_query.shape[0]
    value_heads = dn_value.shape[1] // DV
    query_heads = at_query.shape[1] // HD
    device = lax.axis_index("context")
    row_start = device * tokens_here
    rows = row_start + jnp.arange(tokens_here, dtype=jnp.int32)
    segment, first, prefix, offset, position = row_layout(rows, req_len, req_prefix, req_offset)
    size = lax.axis_size("context")
    query_heads_here = query_heads
    kv_head = lax.axis_index("head") * query_heads_here // (HQ // KVH)
    cosines, sines = yarn_tables(position, ROT)
    new_key = lax.dynamic_slice_in_dim(at_key, kv_head * HD, HD, 1).reshape(tokens_here, 1, HD)
    new_key = (
        rotate(new_key.astype(jnp.float32), cosines, sines, ROT)
        .reshape(tokens_here, HD)
        .astype(jnp.bfloat16)
    )
    new_value = lax.dynamic_slice_in_dim(at_value, kv_head * HD, HD, 1)
    cached_key = lax.dynamic_slice_in_dim(prefix_key, kv_head * HD, HD, 2)
    cached_value = lax.dynamic_slice_in_dim(prefix_value, kv_head * HD, HD, 2)
    states = jnp.stack([prefix_state] + from_others(prefix_state, "context", size, size))
    states = jnp.take(states, (device - jnp.arange(size, dtype=jnp.int32)) % size, axis=0)
    states = jnp.moveaxis(states, 0, 2)
    states = states.reshape(states.shape[:2] + (-1, DK))
    slots_here = cached_key.shape[0]
    own_block = jnp.concatenate(
        [cached_key.reshape(-1, HD), new_key, cached_value.reshape(-1, HD), new_value]
    ).reshape(2, -1, HD)
    block_rows = own_block.shape[1]
    sharers = HQ // KVH // query_heads
    share = block_rows // sharers
    share_index = lax.axis_index("head") % sharers
    mine = lax.dynamic_slice_in_dim(own_block, share_index * share, share, 1)
    received = jnp.stack(from_others(mine, "context", size, size))
    siblings = from_others(received, "head", lax.axis_size("head"), sharers)
    cached_rows = cached_key.shape[0] * cached_key.shape[1]
    square = (value_heads, DK, DK)
    local_out, reach, map_half, carry_add = whole_call(
        local_kernel,
        [
            jax.ShapeDtypeStruct((value_heads, tokens_here, DV), jnp.float32),
            jax.ShapeDtypeStruct((value_heads, tokens_here, DK), jnp.bfloat16),
            jax.ShapeDtypeStruct(square, jnp.bfloat16),
            jax.ShapeDtypeStruct(square, jnp.float32),
        ],
        dn_query,
        dn_key,
        dn_value,
        dn_beta_logit,
        dn_beta_logit.T,
        dn_decay,
        dn_decay.T,
        segment[:, None],
        segment[None, :],
    )
    restarts = first[tokens_here - 1] >= row_start
    tail_prefix = prefix[tokens_here - 1]
    base = jnp.zeros(states.shape[1:], states.dtype)
    for owner in range(states.shape[0]):
        base = jnp.where(tail_prefix == owner, states[owner], base)
    fresh = jnp.einsum("hvj,hjk->hvk", base, map_half, preferred_element_type=jnp.float32)
    into_state = chain(
        jnp.where(restarts, 0, map_half).astype(jnp.bfloat16),
        carry_add + jnp.where(restarts, fresh, 0.0),
        size,
    )
    carried = (segment == segment[0]) & (first[0] < row_start)
    owner_ids = jnp.arange(states.shape[0], dtype=jnp.int32)
    select = (prefix[None, :] == owner_ids[:, None]) & ~carried[None, :]
    select = jnp.concatenate([select, carried[None, :]], axis=0)
    dn_out = whole_call(
        finish_kernel,
        jax.ShapeDtypeStruct((tokens_here, value_heads * DV), jnp.bfloat16),
        local_out,
        reach,
        states,
        into_state,
        select.astype(jnp.float32).T,
        dn_gate,
        dn_norm_gain[None, :],
    )
    blocks_per_prefix = block_table.shape[0] // prefix_state.shape[0]
    width = cached_key.shape[1]
    others = (device - 1 - jnp.arange(size - 1, dtype=jnp.int32)) % size
    origins = [jnp.full((block_rows,), device, jnp.int32)]
    parts = [jnp.arange(block_rows, dtype=jnp.int32)]
    for step in range(sharers):
        origins.append(jnp.repeat(others, share))
        parts.append(
            (share_index - step) % sharers * share
            + jnp.tile(jnp.arange(share, dtype=jnp.int32), size - 1)
        )
    origin, part = jnp.concatenate(origins), jnp.concatenate(parts)
    slot = origin * slots_here + part // width
    entry = jnp.sum(
        jnp.where(
            block_table[:, None] == slot[None, :],
            jnp.arange(block_table.shape[0], dtype=jnp.int32)[:, None],
            0,
        ),
        axis=0,
    )
    key_row = origin * tokens_here + part - cached_rows
    starts = jnp.cumsum(req_len) - req_len
    key_segment = jnp.sum((starts[:, None] <= key_row[None, :]).astype(jnp.int32), axis=0) - 1
    old = part < cached_rows
    prefixes = prefix_state.shape[0]
    code = jnp.where(old, entry // blocks_per_prefix, prefixes + key_segment)
    place = jnp.where(old, entry % blocks_per_prefix * width + part % width, key_row)
    ones = jnp.ones((tokens_here, 128 - ROT), jnp.float32)
    at_out = whole_call(
        attend_kernel,
        jax.ShapeDtypeStruct((tokens_here, query_heads * HD), jnp.bfloat16),
        at_query,
        jnp.concatenate([cosines, cosines, ones], axis=1),
        jnp.concatenate([-sines, sines, 0.0 * ones], axis=1),
        at_gate,
        jnp.stack([prefix, offset, prefixes + segment, rows], axis=1),
        code[None, :],
        place[None, :],
        own_block,
        received,
        *siblings,
    )
    return (dn_out, at_out)


def solution(mesh):
    placed = (
        P(("group", "context"), "head"),
        P(("group", "context"), "head"),
        P(("group", "context"), "head"),
        P(("group", "context"), "head"),
        P(("group", "context"), "head"),
        P(("group", "context"), "head"),
        P(),
        P("group", "head", "context", None),
        P(("group", "context"), "head"),
        P(("group", "context"), "head"),
        P(("group", "context"), None),
        P(("group", "context"), None),
        P(("group", "context"), None, None),
        P(("group", "context"), None, None),
        P("group"),
        P("group"),
        P("group"),
        P("group"),
    )
    return jax.shard_map(
        shards,
        mesh=mesh,
        in_specs=placed,
        out_specs=(P(("group", "context"), "head"), P(("group", "context"), "head")),
        check_vma=False,
    )
```

```python
import math

import jax
import jax.numpy as jnp
from jax import lax
from jax.experimental import pallas as pl
from jax.experimental.pallas import tpu as pltpu
from jax.sharding import PartitionSpec as P

VH = 32
KH = 16
DK = 128
DV = 128
HQ = 16
KVH = 2
HD = 256
ROT = 64


ROPE_THETA = 10000000.0
YARN_FACTOR = 4.0
YARN_ANCHOR = 262144.0
NEG_LARGE = -1e30
HIGH = lax.Precision.HIGHEST


def chain_kernel(size, map_ref, add_ref, into_ref, held, leaving, send_sem, recv_sem):
    me = lax.axis_index("context")
    heads = map_ref.shape[0]
    barrier = pltpu.get_barrier_semaphore()
    after, before = lax.rem(me + 1, size), lax.rem(me + size - 1, size)
    for neighbour in (before, after):
        pl.semaphore_signal(barrier, inc=1, device_id={"context": neighbour})
    pl.semaphore_wait(barrier, 2)

    def sent(h):
        return pltpu.make_async_remote_copy(
            src_ref=leaving.at[h],
            dst_ref=held.at[h],
            send_sem=send_sem.at[h],
            recv_sem=recv_sem.at[h],
            device_id={"context": after},
        )

    @pl.when(me == 0)
    def _():
        held[...] = jnp.zeros_like(held)

    for h in range(heads):

        @pl.when(me > 0)
        def _(h=h):
            sent(h).wait_recv()

        leaving[h] = (
            jnp.dot(held[h], map_ref[h], preferred_element_type=jnp.float32) + add_ref[h]
        ).astype(jnp.bfloat16)

        @pl.when(me < size - 1)
        def _(h=h):
            sent(h).start()

    into_ref[...] = held[...]

    @pl.when(me < size - 1)
    def _():
        for h in range(heads):
            sent(h).wait_send()


def chain(carry_map, carry_add, size):
    heads = carry_map.shape[0]
    return pl.pallas_call(
        lambda *refs: chain_kernel(size, *refs),
        out_shape=jax.ShapeDtypeStruct(carry_add.shape, jnp.bfloat16),
        in_specs=[pl.BlockSpec(memory_space=pltpu.VMEM)] * 2,
        out_specs=pl.BlockSpec(memory_space=pltpu.VMEM),
        scratch_shapes=[
            pltpu.VMEM(carry_add.shape, jnp.bfloat16),
            pltpu.VMEM(carry_add.shape, jnp.bfloat16),
            pltpu.SemaphoreType.DMA((heads,)),
            pltpu.SemaphoreType.DMA((heads,)),
        ],
        compiler_params=pltpu.CompilerParams(collective_id=1, has_side_effects=True),
    )(carry_map, carry_add)


def from_others(x, axis, size, span):
    return [
        lax.ppermute(
            x, axis, [(i, i // span * span + (i + step) % span) for i in range(size)]
        )
        for step in range(1, span)
    ]


def halves(x):
    high = x.astype(jnp.bfloat16)
    return high, (x - high.astype(jnp.float32)).astype(jnp.bfloat16)


def dot1(a, b, contract=((1,), (0,))):
    return lax.dot_general(a, b, (contract, ((), ())), preferred_element_type=jnp.float32)


def dot2(a, exact):
    high, low = halves(a)
    return dot1(high, exact) + dot1(low, exact)


def dot3(a, b):
    a_high, a_low = halves(a)
    b_high, b_low = halves(b)
    return dot1(a_high, b_high) + (dot1(a_high, b_low) + dot1(a_low, b_high))


def local_kernel(
    query_ref, key_ref, value_ref, logit_ref, logit_row_ref, decay_ref, decay_row_ref,
    seg_ref, seg_row_ref, local_ref, reach_ref, map_ref, add_ref,
):
    tokens = query_ref.shape[0]
    heads = local_ref.shape[0]
    share = VH // KH
    seg, seg_row = seg_ref[...], seg_row_ref[...]
    row = lax.broadcasted_iota(jnp.int32, (tokens, tokens), 0)
    col = lax.broadcasted_iota(jnp.int32, (tokens, tokens), 1)
    same = seg == seg_row
    causal = same & (row >= col)
    strict = same & (row > col)
    eye = row == col
    causal_f = causal.astype(jnp.float32)
    run = lax.dot_general(
        causal_f, decay_ref[...], (((1,), (0,)), ((), ())),
        precision=HIGH, preferred_element_type=jnp.float32,
    )
    run_row = lax.dot_general(
        decay_row_ref[...], causal_f, (((1,), (1,)), ((), ())),
        precision=HIGH, preferred_element_type=jnp.float32,
    )
    beta, beta_row = jax.nn.sigmoid(logit_ref[...]), jax.nn.sigmoid(logit_row_ref[...])
    start, start_row = jnp.exp(run), jnp.exp(run_row)
    tail = seg_row == seg_row[:, tokens - 1 : tokens]
    end_row = jnp.where(
        tail, jnp.exp(jnp.where(tail, run_row[:, tokens - 1 : tokens] - run_row, 0.0)), 0.0
    )
    keys, grams, mixes, scaled, inv_rows = [], [], [], [], []
    for g in range(heads // share):
        k = key_ref[:, g * DK : (g + 1) * DK]
        q = query_ref[:, g * DK : (g + 1) * DK]
        gram = dot1(k, k, ((1,), (1,)))
        cross = dot1(q, k, ((1,), (1,)))
        squares = jnp.where(eye, gram, 0.0)
        inv = lax.rsqrt(jnp.sum(squares, axis=1, keepdims=True) + 1e-06)
        inv_row = lax.rsqrt(jnp.sum(squares, axis=0, keepdims=True) + 1e-06)
        q_f = q.astype(jnp.float32)
        inv_q = lax.rsqrt(jnp.sum(q_f * q_f, axis=1, keepdims=True) + 1e-06) * DK ** (-0.5)
        keys.append(k)
        inv_rows.append(inv_row)
        grams.append(gram * inv * inv_row)
        mixes.append(cross * inv_q * inv_row)
        scaled.append(q_f * inv_q)
    lowers, inverses, mixing = [], [], []
    for h in range(heads):
        gaps = run[:, h : h + 1] - run_row[h : h + 1, :]
        decay_mat = jnp.where(causal, jnp.exp(jnp.where(causal, gaps, 0.0)), 0.0)
        mixing.append(decay_mat * mixes[h // share])
        lower = jnp.where(strict, beta[:, h : h + 1] * grams[h // share] * decay_mat, 0.0)
        lowers.append(lower)
        inverses.append(
            jnp.where(eye, 1.0, 0.0) - jnp.where(row // 2 == col // 2, lower, 0.0)
        )
    width = 2
    while width < tokens:
        pair = (row // (2 * width) == col // (2 * width)) & (row // width > col // width)
        half = [dot3(jnp.where(pair, lowers[h], 0.0), inverses[h]) for h in range(heads)]
        inverses = [inverses[h] - dot3(inverses[h], half[h]) for h in range(heads)]
        width *= 2
    for h in range(heads):
        g = h // share
        weighted = inverses[h] * beta_row[h : h + 1, :]
        update = dot2(weighted, value_ref[:, h * DV : (h + 1) * DV])
        wy = dot2(weighted * (start_row[h : h + 1, :] * inv_rows[g]), keys[g])
        solved = jnp.concatenate([update, wy], axis=1)
        mixed = dot3(mixing[h], solved)
        local_ref[h] = mixed[:, :DV]
        reach_ref[h] = (start[:, h : h + 1] * scaled[g] - mixed[:, DV:]).astype(jnp.bfloat16)
        turned = solved.T * (end_row[h : h + 1, :] * inv_rows[g])
        carry = dot2(turned, keys[g])
        add_ref[h] = carry[:DV]
        map_ref[h] = (
            jnp.where(eye, start[tokens - 1 : tokens, h : h + 1], 0.0) - carry[DV:]
        ).astype(jnp.bfloat16)


def finish_kernel(local_ref, reach_ref, states_ref, into_ref, select_ref, gate_ref, gain_ref, out_ref):
    owners = states_ref.shape[0]
    select = select_ref[...] > 0.5
    for h in range(local_ref.shape[0]):
        core = local_ref[h]
        reach = reach_ref[h]
        for owner in range(owners + 1):
            state = states_ref[owner, h] if owner < owners else into_ref[h]
            part = dot1(reach, state, ((1,), (1,)))
            core = core + jnp.where(select[:, owner : owner + 1], part, 0.0)
        normed = core * lax.rsqrt(jnp.mean(core * core, axis=1, keepdims=True) + 1e-06)
        gate = gate_ref[:, h * DV : (h + 1) * DV].astype(jnp.float32)
        out_ref[:, h * DV : (h + 1) * DV] = (
            normed * gain_ref[...] * (gate * jax.nn.sigmoid(gate))
        ).astype(jnp.bfloat16)


def attend_kernel(
    query_ref, cos_ref, sin_ref, gate_ref, row_ref, code_ref, place_ref, own_ref, *rest
):
    pieces, out_ref = [own_ref] + list(rest[:-1]), rest[-1]
    tokens = query_ref.shape[0]
    cosines, sines = cos_ref[...], sin_ref[...]
    lane = lax.broadcasted_iota(jnp.int32, (tokens, 128), 1)
    old_code, limit = row_ref[:, 0:1], row_ref[:, 1:2]
    new_code, own_row = row_ref[:, 2:3], row_ref[:, 3:4]
    keys, values, seen, at = [], [], [], 0
    for ref in pieces:
        if len(ref.shape) == 3:
            keys.append(ref[0])
            values.append(ref[1])
        else:
            keys.append(ref[:, 0].reshape(-1, HD))
            values.append(ref[:, 1].reshape(-1, HD))
        count = keys[-1].shape[0]
        code, place = code_ref[:, at : at + count], place_ref[:, at : at + count]
        at += count
        seen.append(
            ((code == old_code) & (place < limit)) | ((code == new_code) & (place <= own_row))
        )
    for h in range(query_ref.shape[1] // HD):
        front = query_ref[:, h * HD : h * HD + 128].astype(jnp.float32)
        swapped = jnp.where(
            lane < ROT // 2, pltpu.roll(front, 128 - ROT // 2, 1), pltpu.roll(front, ROT // 2, 1)
        )
        query = jnp.concatenate(
            [
                (front * cosines + swapped * sines).astype(jnp.bfloat16),
                query_ref[:, h * HD + 128 : (h + 1) * HD],
            ],
            axis=1,
        )
        scores = [
            jnp.where(see, dot1(query, key, ((1,), (1,))) * HD ** (-0.5), NEG_LARGE)
            for see, key in zip(seen, keys)
        ]
        peak = jnp.max(scores[0], axis=1, keepdims=True)
        for score in scores[1:]:
            peak = jnp.maximum(peak, jnp.max(score, axis=1, keepdims=True))
        total, summed = 0.0, 0.0
        for score, see, value in zip(scores, seen, values):
            weight = jnp.where(see, jnp.exp(score - peak), 0.0)
            total = total + jnp.sum(weight, axis=1, keepdims=True)
            summed = summed + dot1(weight.astype(jnp.bfloat16), value)
        gate = gate_ref[:, h * HD : (h + 1) * HD].astype(jnp.float32)
        out_ref[:, h * HD : (h + 1) * HD] = (
            summed / total * jax.nn.sigmoid(gate)
        ).astype(jnp.bfloat16)


def whole_call(kernel, shapes, *arrays):
    space = pl.BlockSpec(memory_space=pltpu.VMEM)
    return pl.pallas_call(
        kernel,
        out_shape=shapes,
        in_specs=[space] * len(arrays),
        out_specs=jax.tree.map(lambda _: space, shapes),
        compiler_params=pltpu.CompilerParams(vmem_limit_bytes=48 * 2**20),
    )(*arrays)


def yarn_tables(positions, rotary):
    half = rotary // 2
    log_theta = math.log(ROPE_THETA)
    lower = max(
        math.floor(rotary * math.log(YARN_ANCHOR / (64.0 * math.pi)) / (2.0 * log_theta)), 0
    )
    upper = min(
        math.ceil(rotary * math.log(YARN_ANCHOR / (2.0 * math.pi)) / (2.0 * log_theta)), rotary - 1
    )
    spread = float(upper - lower)
    index = jnp.arange(half, dtype=jnp.float32)
    plain_frequency = jnp.exp(index * (-2.0 * log_theta / rotary))
    keep = 1.0 - jnp.clip((index - lower) / spread, 0.0, 1.0)
    frequency = plain_frequency * keep + plain_frequency / YARN_FACTOR * (1.0 - keep)
    angles = positions.astype(jnp.float32)[:, None] * frequency[None, :]
    attention_factor = 0.1 * math.log(YARN_FACTOR) + 1.0
    return (jnp.cos(angles) * attention_factor, jnp.sin(angles) * attention_factor)


def rotate(values, cosines, sines, rotary):
    half = rotary // 2
    first = values[..., :half]
    second = values[..., half:rotary]
    cosines = cosines[:, None, :]
    sines = sines[:, None, :]
    return jnp.concatenate(
        [first * cosines - second * sines, second * cosines + first * sines, values[..., rotary:]],
        axis=-1,
    )


def row_layout(rows, req_len, req_prefix, req_offset):
    starts = jnp.cumsum(req_len) - req_len
    leading_found = (starts[None, :] <= rows[:, None]).astype(jnp.int32)
    segment = jnp.sum(leading_found, axis=1) - 1
    choose = (segment[:, None] == jnp.arange(req_len.shape[0], dtype=jnp.int32)[None, :]).astype(
        jnp.int32
    )
    first = jnp.sum(choose * starts[None, :], axis=1)
    prefix = jnp.sum(choose * req_prefix[None, :], axis=1)
    offset = jnp.sum(choose * req_offset[None, :], axis=1)
    return (segment, first, prefix, offset, offset + rows - first)


def shards(
    dn_query,
    dn_key,
    dn_value,
    dn_gate,
    dn_beta_logit,
    dn_decay,
    dn_norm_gain,
    prefix_state,
    at_query,
    at_gate,
    at_key,
    at_value,
    prefix_key,
    prefix_value,
    req_len,
    req_prefix,
    req_offset,
    block_table,
):
    tokens_here = dn_query.shape[0]
    value_heads = dn_value.shape[1] // DV
    query_heads = at_query.shape[1] // HD
    device = lax.axis_index("context")
    row_start = device * tokens_here
    rows = row_start + jnp.arange(tokens_here, dtype=jnp.int32)
    segment, first, prefix, offset, position = row_layout(rows, req_len, req_prefix, req_offset)
    size = lax.axis_size("context")
    query_heads_here = query_heads
    kv_head = lax.axis_index("head") * query_heads_here // (HQ // KVH)
    cosines, sines = yarn_tables(position, ROT)
    new_key = lax.dynamic_slice_in_dim(at_key, kv_head * HD, HD, 1).reshape(tokens_here, 1, HD)
    new_key = (
        rotate(new_key.astype(jnp.float32), cosines, sines, ROT)
        .reshape(tokens_here, HD)
        .astype(jnp.bfloat16)
    )
    new_value = lax.dynamic_slice_in_dim(at_value, kv_head * HD, HD, 1)
    cached_key = lax.dynamic_slice_in_dim(prefix_key, kv_head * HD, HD, 2)
    cached_value = lax.dynamic_slice_in_dim(prefix_value, kv_head * HD, HD, 2)
    turned = from_others(prefix_state, "context", size, size)
    states = jnp.stack([prefix_state] + turned)
    states = jnp.take(
        states, (device - jnp.arange(size, dtype=jnp.int32)) % size, axis=0, mode="clip"
    )
    states = jnp.moveaxis(states, 0, 2)
    states = states.reshape(states.shape[:2] + (-1, DK))
    slots_here = cached_key.shape[0]
    own_block = jnp.concatenate(
        [cached_key.reshape(-1, HD), new_key, cached_value.reshape(-1, HD), new_value]
    ).reshape(2, -1, HD)
    block_rows = own_block.shape[1]
    sharers = HQ // KVH // query_heads
    share = block_rows // sharers
    share_index = lax.axis_index("head") % sharers
    mine = lax.dynamic_slice_in_dim(own_block, share_index * share, share, 1)
    mine = lax.optimization_barrier((mine, turned[0]))[0]
    received = jnp.stack(from_others(mine, "context", size, size))
    siblings = from_others(received, "head", lax.axis_size("head"), sharers)
    cached_rows = cached_key.shape[0] * cached_key.shape[1]
    square = (value_heads, DK, DK)
    local_out, reach, map_half, carry_add = whole_call(
        local_kernel,
        [
            jax.ShapeDtypeStruct((value_heads, tokens_here, DV), jnp.float32),
            jax.ShapeDtypeStruct((value_heads, tokens_here, DK), jnp.bfloat16),
            jax.ShapeDtypeStruct(square, jnp.bfloat16),
            jax.ShapeDtypeStruct(square, jnp.float32),
        ],
        dn_query,
        dn_key,
        dn_value,
        dn_beta_logit,
        dn_beta_logit.T,
        dn_decay,
        dn_decay.T,
        segment[:, None],
        segment[None, :],
    )
    restarts = first[tokens_here - 1] >= row_start
    tail_prefix = prefix[tokens_here - 1]
    base = jnp.zeros(states.shape[1:], states.dtype)
    for owner in range(states.shape[0]):
        base = jnp.where(tail_prefix == owner, states[owner], base)
    fresh = jnp.einsum("hvj,hjk->hvk", base, map_half, preferred_element_type=jnp.float32)
    into_state = chain(
        jnp.where(restarts, 0, map_half).astype(jnp.bfloat16),
        carry_add + jnp.where(restarts, fresh, 0.0),
        size,
    )
    carried = (segment == segment[0]) & (first[0] < row_start)
    owner_ids = jnp.arange(states.shape[0], dtype=jnp.int32)
    select = (prefix[None, :] == owner_ids[:, None]) & ~carried[None, :]
    select = jnp.concatenate([select, carried[None, :]], axis=0)
    dn_out = whole_call(
        finish_kernel,
        jax.ShapeDtypeStruct((tokens_here, value_heads * DV), jnp.bfloat16),
        local_out,
        reach,
        states,
        into_state,
        select.astype(jnp.float32).T,
        dn_gate,
        dn_norm_gain[None, :],
    )
    blocks_per_prefix = block_table.shape[0] // prefix_state.shape[0]
    width = cached_key.shape[1]
    others = (device - 1 - jnp.arange(size - 1, dtype=jnp.int32)) % size
    origins = [jnp.full((block_rows,), device, jnp.int32)]
    parts = [jnp.arange(block_rows, dtype=jnp.int32)]
    for step in range(sharers):
        origins.append(jnp.repeat(others, share))
        parts.append(
            (share_index - step) % sharers * share
            + jnp.tile(jnp.arange(share, dtype=jnp.int32), size - 1)
        )
    origin, part = jnp.concatenate(origins), jnp.concatenate(parts)
    slot = origin * slots_here + part // width
    entry = jnp.sum(
        jnp.where(
            block_table[:, None] == slot[None, :],
            jnp.arange(block_table.shape[0], dtype=jnp.int32)[:, None],
            0,
        ),
        axis=0,
    )
    key_row = origin * tokens_here + part - cached_rows
    starts = jnp.cumsum(req_len) - req_len
    key_segment = jnp.sum((starts[:, None] <= key_row[None, :]).astype(jnp.int32), axis=0) - 1
    old = part < cached_rows
    prefixes = prefix_state.shape[0]
    code = jnp.where(old, entry // blocks_per_prefix, prefixes + key_segment)
    place = jnp.where(old, entry % blocks_per_prefix * width + part % width, key_row)
    ones = jnp.ones((tokens_here, 128 - ROT), jnp.float32)
    at_out = whole_call(
        attend_kernel,
        jax.ShapeDtypeStruct((tokens_here, query_heads * HD), jnp.bfloat16),
        at_query,
        jnp.concatenate([cosines, cosines, ones], axis=1),
        jnp.concatenate([-sines, sines, 0.0 * ones], axis=1),
        at_gate,
        jnp.stack([prefix, offset, prefixes + segment, rows], axis=1),
        code[None, :],
        place[None, :],
        own_block,
        received,
        *siblings,
    )
    return (dn_out, at_out)


def solution(mesh):
    placed = (
        P(("group", "context"), "head"),
        P(("group", "context"), "head"),
        P(("group", "context"), "head"),
        P(("group", "context"), "head"),
        P(("group", "context"), "head"),
        P(("group", "context"), "head"),
        P(),
        P("group", "head", "context", None),
        P(("group", "context"), "head"),
        P(("group", "context"), "head"),
        P(("group", "context"), None),
        P(("group", "context"), None),
        P(("group", "context"), None, None),
        P(("group", "context"), None, None),
        P("group"),
        P("group"),
        P("group"),
        P("group"),
    )
    return jax.shard_map(
        shards,
        mesh=mesh,
        in_specs=placed,
        out_specs=(P(("group", "context"), "head"), P(("group", "context"), "head")),
        check_vma=False,
    )
```
